32 devices in a mesh: dp: 4 (over y, x), seq: 8 (over z, core).
Axes of the slice: x: 2, y: 2, z: 4, core: 2. Of those that a mesh axis runs over, the one named last changes fastest.
Arguments:
- stream: bfloat16 [4, 1024, 512], P('dp', 'seq'), may hold values from -6 to 6
- byte_ids: int32 [4, 1024], P('dp', 'seq'), may hold values from 0 to 255
- cotangent: bfloat16 [4, 1024, 512], P('dp', 'seq'), may hold values from -6 to 6
- embed_flat: bfloat16 [131072], P(('dp', 'seq')), may hold values from -6 to 6
- qkv_flat: bfloat16 [786432], P(('dp', 'seq')), may hold values from -0.25 to 0.25
- out_flat: bfloat16 [262144], P(('dp', 'seq')), may hold values from -6 to 6
- up_flat: bfloat16 [1048576], P(('dp', 'seq')), may hold values from -0.25 to 0.25
- down_flat: bfloat16 [1048576], P(('dp', 'seq')), may hold values from -0.125 to 0.125
- gains: bfloat16 [1024], P(('dp', 'seq')), may hold values from 0.5 to 1.5
- norm_shifts: bfloat16 [1024], P(('dp', 'seq')), may hold values from -2 to 2
- out_shifts: bfloat16 [1024], P(('dp', 'seq')), may hold values from -2 to 2
- up_bias: bfloat16 [2048], P(('dp', 'seq')), may hold values from -2 to 2
- rel_bias: bfloat16 [256], P(('dp', 'seq')), may hold values from -4 to 4
Outputs:
- activations: bfloat16 [4, 1024, 512], P('dp', 'seq')
- grad_stream: bfloat16 [4, 1024, 512], P('dp', 'seq')
- grad_embed: float32 [131072], P(('dp', 'seq'))
- grad_qkv: float32 [786432], P(('dp', 'seq'))
- grad_out_weight: float32 [262144], P(('dp', 'seq'))
- grad_up: float32 [1048576], P(('dp', 'seq'))
- grad_down: float32 [1048576], P(('dp', 'seq'))
- grad_gains: float32 [1024], P(('dp', 'seq'))
- grad_norm_shifts: float32 [1024], P(('dp', 'seq'))
- grad_out_shifts: float32 [1024], P(('dp', 'seq'))
- grad_up_bias: float32 [2048], P(('dp', 'seq'))
- grad_rel: float32 [256], P(('dp', 'seq'))
The draws below stay inside these ranges and needn't reach their ends.
All inputs are finite; a program needn't handle non-finite values.
Results may differ from the reference program's by a relative error of at most 0.01.
Values may be sent and summed in bfloat16 or wider, within the bound.
A program may use at most 192 MiB of HBM per device.

```python
import math
import jax
import jax.numpy as jnp
import numpy as np
from jax import lax

D = 512
HEADS = 8
HEAD_DIM = 64
FF = 2048
VOCAB = 256
BLOCK = 256
BUCKETS = 32
LEN = 1024
SEQ_ALL = 4


def plant(array, own_key, low, top_value):
    longest = array.shape.index(max(array.shape))
    spots = []
    for shift in (0, 1):
        where = [jax.random.randint(jax.random.fold_in(own_key, axis), (), 0, length) for axis, length in enumerate(array.shape)]
        where[longest] = (where[longest] + shift) % array.shape[longest]
        spots.append(tuple(where))
    return array.at[spots[0]].set(low).at[spots[1]].set(top_value)


def levels(key, shape, pieces, low, high):
    gain, own = 1.0, jax.random.fold_in(key, 6)
    for axis_at, parts in pieces:
        draws = jnp.exp(jax.random.uniform(jax.random.fold_in(own, axis_at), (parts,), jnp.float32, low / len(pieces), high / len(pieces)))
        gain = gain * jnp.repeat(draws, shape[axis_at] // parts).reshape([-1 if axis == axis_at else 1 for axis in range(len(shape))])
    return gain


def rank_bounds(number_of, slope):
    loads = [(1 << 20) // math.isqrt(grade ** slope) + 1 for grade in range(1, number_of + 1)]
    width = 1 + sum(loads) // (1 << 30)
    return np.cumsum(np.array([max(1, weight // width) for weight in loads]))


def skewed_ids(stream_key, dims, number_of, lean):
    listing = rank_bounds(number_of, lean)
    lot = jax.random.randint(jax.random.fold_in(stream_key, 1), dims, 0, int(listing[number_of - 1]))
    grade = jnp.searchsorted(jnp.asarray(listing, jnp.int32), lot, side="right")
    return jax.random.permutation(jax.random.fold_in(stream_key, 2), number_of)[grade].astype(jnp.int32)


def normal_values(own_key, extent, scale, most, cuts=(), kind=jnp.bfloat16):
    gain = levels(own_key, extent, cuts, -0.22, 0.18) if cuts else 1.0
    values = jax.random.normal(own_key, extent, jnp.float32) * scale * gain
    return jnp.minimum(jnp.maximum(values, -most), most).astype(kind)


def setup_inputs(seed: int = 0) -> dict:
    key_of = jax.random.split(jax.random.key(seed), 14)
    stream = normal_values(key_of[0], (SEQ_ALL, LEN, D), 1.0, 6.0, ((0, 4), (1, 8)))
    byte_ids = plant(skewed_ids(key_of[1], (SEQ_ALL, LEN), VOCAB, 2), jax.random.fold_in(key_of[1], 3), 0, VOCAB - 1).astype(jnp.int32)
    cotangent = normal_values(key_of[2], (SEQ_ALL, LEN, D), 1.0, 6.0, ((0, 4), (1, 8)))
    embed_flat = normal_values(key_of[3], (VOCAB * D,), 1.0, 6.0, ((0, 32),))
    qkv_flat = normal_values(key_of[4], (3 * D * D,), D ** -0.5, 0.25, ((0, 32),))
    out_flat = normal_values(key_of[5], (D * D,), (max(1, 2 * D // LEN)) ** -0.5, 6.0, ((0, 32),))
    up_flat = normal_values(key_of[6], (D * FF,), D ** -0.5, 0.25, ((0, 32),))
    down_flat = normal_values(key_of[7], (FF * D,), FF ** -0.5, 0.125, ((0, 32),))
    gains = jnp.clip(1.0 + 0.1 * jax.random.normal(key_of[8], (2 * D,), jnp.float32), 0.5, 1.5).astype(jnp.bfloat16)
    norm_shifts = normal_values(key_of[9], (2 * D,), 0.3, 2.0, ((0, 32),))
    out_shifts = normal_values(key_of[10], (2 * D,), 0.3, 2.0, ((0, 32),))
    up_bias = normal_values(key_of[11], (FF,), 0.3, 2.0, ((0, 32),))
    rel_bias = normal_values(key_of[12], (HEADS * BUCKETS,), 1.0, 4.0, ((0, 32),))
    return dict(stream=stream, byte_ids=byte_ids, cotangent=cotangent, embed_flat=embed_flat, qkv_flat=qkv_flat, out_flat=out_flat, up_flat=up_flat, down_flat=down_flat, gains=gains, norm_shifts=norm_shifts, out_shifts=out_shifts, up_bias=up_bias, rel_bias=rel_bias)


EPSILON = 1e-05
SCALING = 0.125
MASKED = -1e+30

@jax.custom_vjp
def low(v):
    return lax.optimization_barrier(v.astype(jnp.bfloat16)).astype(jnp.float32)

@jax.custom_vjp
def low_back(v):
    return v

def low_keep(v):
    return (low(v), None)

def low_pass(kept, grad):
    return (grad,)

def back_keep(v):
    return (v, None)

def back_low(kept, grad):
    return (low(grad),)
low.defvjp(low_keep, low_pass)
low_back.defvjp(back_keep, back_low)

def layer_norm(hidden, gain_row, shift_row):
    centered = hidden - lax.optimization_barrier(jnp.mean(hidden, axis=-1, keepdims=True))
    spread = lax.optimization_barrier(jnp.mean(centered * centered, axis=-1, keepdims=True))
    return centered * lax.rsqrt(spread + EPSILON) * gain_row + shift_row

def one_sequence(weights, stream_seq, byte_seq):
    embed, w_qkv, w_out, w_up, w_down, gain_pair, norm_pair, out_pair, bias_up, rel_table = weights
    seq_length = stream_seq.shape[0]
    picker = (byte_seq[:, None] == jnp.arange(VOCAB, dtype=jnp.int32)[None, :]).astype(jnp.float32)
    start_rows = stream_seq + jnp.dot(picker, embed, precision=lax.Precision.HIGHEST)
    normed_one = low(layer_norm(start_rows, gain_pair[0], norm_pair[0]))
    projected = low_back(low(jnp.dot(normed_one, w_qkv, precision=lax.Precision.HIGHEST)))
    queries = projected[:, :D].reshape(seq_length, HEADS, HEAD_DIM)
    key_rows = projected[:, D:2 * D].reshape(seq_length, HEADS, HEAD_DIM)
    value_rows = projected[:, 2 * D:].reshape(seq_length, HEADS, HEAD_DIM)
    block_rows = min(512, seq_length)
    key_block = jnp.arange(seq_length, dtype=jnp.int32) // BLOCK

    def attend_rows(first_row):
        query_rows = lax.dynamic_slice_in_dim(queries, first_row, block_rows, 0)
        raw_scores = jnp.einsum('qhd,khd->hqk', query_rows, key_rows, precision=lax.Precision.HIGHEST) * SCALING
        row_block = (first_row + jnp.arange(block_rows, dtype=jnp.int32)) // BLOCK
        distance = row_block[:, None] - key_block[None, :]
        bias_rows = rel_table[:, jnp.clip(distance, 0, BUCKETS - 1)]
        scores = jnp.where(distance[None] >= 0, low_back(raw_scores) + bias_rows, MASKED)
        soft_weights = low(jax.nn.softmax(scores, axis=-1))
        return jnp.einsum('hqk,khd->qhd', soft_weights, value_rows, precision=lax.Precision.HIGHEST)
    firsts = jnp.arange(seq_length // block_rows, dtype=jnp.int32) * block_rows
    mixed = lax.map(jax.checkpoint(attend_rows), firsts).reshape(seq_length, D)
    mixed = low_back(low(mixed))
    middle = start_rows + low_back(jnp.dot(mixed, w_out, precision=lax.Precision.HIGHEST)) + out_pair[0]
    normed_two = low(layer_norm(middle, gain_pair[1], norm_pair[1]))
    lifted = low_back(jnp.dot(normed_two, w_up, precision=lax.Precision.HIGHEST)) + bias_up
    active = low(jax.nn.gelu(lifted, approximate=False))
    return middle + low_back(jnp.dot(active, w_down, precision=lax.Precision.HIGHEST)) + out_pair[1]

def reference(stream, byte_ids, cotangent, embed_flat, qkv_flat, out_flat, up_flat, down_flat, gains, norm_shifts, out_shifts, up_bias, rel_bias):
    weights = (embed_flat.astype(jnp.float32).reshape(VOCAB, D), qkv_flat.astype(jnp.float32).reshape(D, 3 * D), out_flat.astype(jnp.float32).reshape(D, D), up_flat.astype(jnp.float32).reshape(D, FF), down_flat.astype(jnp.float32).reshape(FF, D), gains.astype(jnp.float32).reshape(2, D), norm_shifts.astype(jnp.float32).reshape(2, D), out_shifts.astype(jnp.float32).reshape(2, D), up_bias.astype(jnp.float32), rel_bias.astype(jnp.float32).reshape(HEADS, BUCKETS))

    def forward(stream_all, weight_set):

        def step(carry, operands):
            return (carry, one_sequence(weight_set, operands[0], operands[1]))
        unused_carry, result = lax.scan(step, jnp.zeros((), jnp.float32), (stream_all, byte_ids))
        return result
    result, pull = jax.vjp(forward, stream.astype(jnp.float32), weights)
    grad_input, grad_weights = pull(cotangent.astype(jnp.float32))
    return (result.astype(jnp.bfloat16), grad_input.astype(jnp.bfloat16), grad_weights[0].reshape(-1), grad_weights[1].reshape(-1), grad_weights[2].reshape(-1), grad_weights[3].reshape(-1), grad_weights[4].reshape(-1), grad_weights[5].reshape(-1), grad_weights[6].reshape(-1), grad_weights[7].reshape(-1), grad_weights[8].reshape(-1), grad_weights[9].reshape(-1))
```

```python
import types

import jax
import jax.numpy as jnp
from jax import lax
from jax.experimental import pallas as pl
from jax.experimental.pallas import tpu as pltpu
from jax.sharding import PartitionSpec as P

D = 512
HEADS = 8
HEAD_DIM = 64
FF = 2048
VOCAB = 256
BLOCK = 256
BUCKETS = 32


EPSILON = 1e-05
SCALING = 0.125
MASKED = -1e30


def layer_norm(hidden, gain_row, shift_row):
    centered = hidden - jnp.mean(hidden, axis=-1, keepdims=True)
    spread = jnp.mean(centered * centered, axis=-1, keepdims=True)
    return centered * lax.rsqrt(spread + EPSILON) * gain_row + shift_row


def gelu_exact(values):
    return jax.nn.gelu(values, approximate=False)


def unpack(gathered):
    embed, w_qkv, w_out, w_up, w_down, gain_flat, norm_flat, out_flat, bias_flat, rel_flat = (
        gathered
    )
    return (
        embed.reshape(VOCAB, D),
        w_qkv.reshape(D, 3 * D),
        w_out.reshape(D, D),
        w_up.reshape(D, FF),
        w_down.reshape(FF, D),
        gain_flat.astype(jnp.float32).reshape(2, D),
        norm_flat.astype(jnp.float32).reshape(2, D),
        out_flat.astype(jnp.float32).reshape(2, D),
        bias_flat.astype(jnp.float32),
        rel_flat.astype(jnp.float32).reshape(HEADS, BUCKETS),
    )


def block_terms(rel_table, row_first, row_count, key_first, key_count):
    row_blocks = max(row_count // BLOCK, 1)
    key_blocks = max(key_count // BLOCK, 1)
    row_ids = row_first // BLOCK + jnp.arange(row_blocks, dtype=jnp.int32)
    key_ids = key_first // BLOCK + jnp.arange(key_blocks, dtype=jnp.int32)
    distance = row_ids[:, None] - key_ids[None, :]
    allowed = distance >= 0
    bucket = jnp.clip(distance, 0, BUCKETS - 1)
    selector = (bucket[:, :, None] == jnp.arange(BUCKETS, dtype=jnp.int32)[None, None, :]).astype(
        jnp.float32
    )
    bias_tiles = jnp.einsum("abn,hn->hab", selector, rel_table, precision=lax.Precision.HIGHEST)
    return (bias_tiles, allowed, selector)


def score_tile(query_heads, key_heads, bias_tiles, allowed):
    row_count = query_heads.shape[0]
    key_count = key_heads.shape[0]
    raw_scores = (
        jnp.einsum("qhd,khd->hqk", query_heads, key_heads, preferred_element_type=jnp.float32)
        * SCALING
    )
    row_blocks = bias_tiles.shape[1]
    key_blocks = bias_tiles.shape[2]
    tiled = raw_scores.reshape(
        HEADS, row_blocks, row_count // row_blocks, key_blocks, key_count // key_blocks
    )
    tiled = tiled + bias_tiles[:, :, None, :, None]
    tiled = jnp.where(allowed[None, :, None, :, None], tiled, MASKED)
    return tiled.reshape(HEADS, row_count, key_count)


def heads_of(rows):
    return rows.reshape(rows.shape[0], HEADS, HEAD_DIM)


def attend(queries, key_rows, value_rows, bias_tiles, allowed):
    local_rows = queries.shape[0]
    scores = score_tile(heads_of(queries), heads_of(key_rows), bias_tiles, allowed)
    row_max = jnp.max(scores, axis=-1, keepdims=True)
    shifted = jnp.exp(scores - row_max)
    row_sum = jnp.sum(shifted, axis=-1, keepdims=True)
    soft_weights = (shifted / row_sum).astype(jnp.bfloat16)
    mixed_heads = jnp.einsum(
        "hqk,khd->qhd", soft_weights, heads_of(value_rows), preferred_element_type=jnp.float32
    )
    return (mixed_heads.reshape(local_rows, D), (row_max + jnp.log(row_sum))[:, :, 0])


def row_back(queries, key_rows, value_rows, log_totals, grad_mixed, bias_tiles, allowed, selector):
    local_rows = queries.shape[0]
    seq_length = key_rows.shape[0]
    query_heads = heads_of(queries)
    key_heads = heads_of(key_rows)
    value_heads = heads_of(value_rows)
    grad_heads = heads_of(grad_mixed)
    scores = score_tile(query_heads, key_heads, bias_tiles, allowed)
    soft_weights = jnp.exp(scores - log_totals[:, :, None])
    grad_weights = jnp.einsum(
        "qhd,khd->hqk", grad_heads, value_heads, preferred_element_type=jnp.float32
    )
    row_inner = jnp.sum(soft_weights * grad_weights, axis=-1)
    grad_scores = soft_weights * (grad_weights - row_inner[:, :, None])
    row_blocks = bias_tiles.shape[1]
    key_blocks = bias_tiles.shape[2]
    tile_sums = jnp.sum(
        grad_scores.reshape(
            HEADS, row_blocks, local_rows // row_blocks, key_blocks, seq_length // key_blocks
        ),
        axis=(2, 4),
    )
    grad_table = jnp.einsum("hab,abn->hn", tile_sums, selector, precision=lax.Precision.HIGHEST)
    scores_low = grad_scores.astype(jnp.bfloat16)
    grad_queries = (
        jnp.einsum("hqk,khd->qhd", scores_low, key_heads, preferred_element_type=jnp.float32)
        * SCALING
    )
    grad_queries = grad_queries.reshape(local_rows, D)
    grad_keys = (
        jnp.einsum("hqk,qhd->khd", scores_low, query_heads, preferred_element_type=jnp.float32)
        * SCALING
    )
    grad_values = jnp.einsum(
        "hqk,qhd->khd",
        soft_weights.astype(jnp.bfloat16),
        grad_heads,
        preferred_element_type=jnp.float32,
    )
    return (
        grad_queries,
        grad_table,
        row_inner,
        grad_keys.reshape(seq_length, D),
        grad_values.reshape(seq_length, D),
    )


def local(
    stream,
    byte_ids,
    cotangent,
    embed_flat,
    qkv_flat,
    out_flat,
    up_flat,
    down_flat,
    gains,
    norm_shifts,
    out_shifts,
    up_bias,
    rel_bias,
):
    seq_count = stream.shape[0]
    local_rows = stream.shape[1]
    seq_length = local_rows * lax.axis_size("seq")
    tokens = seq_count * local_rows
    first_row = lax.axis_index("seq") * local_rows
    owned = (
        embed_flat,
        qkv_flat,
        out_flat,
        up_flat,
        down_flat,
        gains,
        norm_shifts,
        out_shifts,
        up_bias,
        rel_bias,
    )
    gathered = (
        lax.all_gather(owned[0], ("dp", "seq"), axis=0, tiled=True),
        lax.all_gather(owned[1], ("dp", "seq"), axis=0, tiled=True),
        lax.all_gather(owned[2], ("dp", "seq"), axis=0, tiled=True),
        lax.all_gather(owned[3], ("dp", "seq"), axis=0, tiled=True),
        lax.all_gather(owned[4], ("dp", "seq"), axis=0, tiled=True),
        lax.all_gather(owned[5], ("dp", "seq"), axis=0, tiled=True),
        lax.all_gather(owned[6], ("dp", "seq"), axis=0, tiled=True),
        lax.all_gather(owned[7], ("dp", "seq"), axis=0, tiled=True),
        lax.all_gather(owned[8], ("dp", "seq"), axis=0, tiled=True),
        lax.all_gather(owned[9], ("dp", "seq"), axis=0, tiled=True),
    )
    embed, w_qkv, w_out, w_up, w_down, gain_pair, norm_pair, out_pair, bias_up, rel_table = unpack(
        gathered
    )
    picker = byte_ids.reshape(tokens, 1) == jnp.arange(VOCAB, dtype=jnp.int32)[None, :]
    embedded = jnp.dot(picker.astype(jnp.bfloat16), embed, preferred_element_type=jnp.float32)
    start_rows = stream.reshape(tokens, D).astype(jnp.float32) + embedded
    normed_wide, norm_back_one = jax.vjp(layer_norm, start_rows, gain_pair[0], norm_pair[0])
    normed_one = normed_wide.astype(jnp.bfloat16)
    projected = jnp.dot(normed_one, w_qkv, preferred_element_type=jnp.float32).astype(jnp.bfloat16)
    queries = projected[:, :D].reshape(seq_count, local_rows, D)
    key_rows = projected[:, D : 2 * D].reshape(seq_count, local_rows, D)
    value_rows = projected[:, 2 * D :].reshape(seq_count, local_rows, D)
    keys_all, values_all = (
        lax.all_gather(key_rows, "seq", axis=1, tiled=True),
        lax.all_gather(value_rows, "seq", axis=1, tiled=True),
    )
    bias_tiles, allowed, selector = block_terms(rel_table, first_row, local_rows, 0, seq_length)

    def attend_single(operands):
        return attend(operands[0], operands[1], operands[2], bias_tiles, allowed)

    mixed, log_totals = lax.map(attend_single, (queries, keys_all, values_all))
    mixed_low = mixed.reshape(tokens, D).astype(jnp.bfloat16)
    middle = (
        start_rows + jnp.dot(mixed_low, w_out, preferred_element_type=jnp.float32) + out_pair[0]
    )
    normed_mid, norm_back_two = jax.vjp(layer_norm, middle, gain_pair[1], norm_pair[1])
    normed_two = normed_mid.astype(jnp.bfloat16)
    lifted = jnp.dot(normed_two, w_up, preferred_element_type=jnp.float32) + bias_up
    activated, gelu_back = jax.vjp(gelu_exact, lifted)
    active = activated.astype(jnp.bfloat16)
    result = middle + jnp.dot(active, w_down, preferred_element_type=jnp.float32) + out_pair[1]
    gathered_again = (
        lax.all_gather(owned[0], ("dp", "seq"), axis=0, tiled=True),
        lax.all_gather(owned[1], ("dp", "seq"), axis=0, tiled=True),
        lax.all_gather(owned[2], ("dp", "seq"), axis=0, tiled=True),
        lax.all_gather(owned[3], ("dp", "seq"), axis=0, tiled=True),
        lax.all_gather(owned[4], ("dp", "seq"), axis=0, tiled=True),
        lax.all_gather(owned[5], ("dp", "seq"), axis=0, tiled=True),
        lax.all_gather(owned[6], ("dp", "seq"), axis=0, tiled=True),
        lax.all_gather(owned[7], ("dp", "seq"), axis=0, tiled=True),
        lax.all_gather(owned[8], ("dp", "seq"), axis=0, tiled=True),
        lax.all_gather(owned[9], ("dp", "seq"), axis=0, tiled=True),
    )
    embed, w_qkv, w_out, w_up, w_down, gain_pair, norm_pair, out_pair, bias_up, rel_table = unpack(
        gathered_again
    )
    grad_output = cotangent.reshape(tokens, D)
    grad_wide = grad_output.astype(jnp.float32)
    grad_shift_down = jnp.sum(grad_wide, axis=0)
    grad_w_down = jnp.einsum("tf,td->fd", active, grad_output, preferred_element_type=jnp.float32)
    grad_active = jnp.einsum("td,fd->tf", grad_output, w_down, preferred_element_type=jnp.float32)
    (grad_lifted,) = gelu_back(grad_active)
    grad_bias_up = jnp.sum(grad_lifted, axis=0)
    lifted_low = grad_lifted.astype(jnp.bfloat16)
    grad_w_up = jnp.einsum("td,tf->df", normed_two, lifted_low, preferred_element_type=jnp.float32)
    grad_normed_two = jnp.einsum("tf,df->td", lifted_low, w_up, preferred_element_type=jnp.float32)
    grad_mid_norm, grad_gain_two, grad_shift_two = norm_back_two(grad_normed_two)
    grad_middle = grad_wide + grad_mid_norm
    grad_shift_out = jnp.sum(grad_middle, axis=0)
    middle_low = grad_middle.astype(jnp.bfloat16)
    grad_w_out = jnp.einsum("te,td->ed", mixed_low, middle_low, preferred_element_type=jnp.float32)
    grad_mixed = jnp.einsum("td,ed->te", middle_low, w_out, preferred_element_type=jnp.float32)
    grad_mixed = grad_mixed.astype(jnp.bfloat16).reshape(seq_count, local_rows, D)
    keys_all, values_all = (
        lax.all_gather(key_rows, "seq", axis=1, tiled=True),
        lax.all_gather(value_rows, "seq", axis=1, tiled=True),
    )

    def back_with_keys(operands):
        return row_back(
            operands[0],
            operands[1],
            operands[2],
            operands[3],
            operands[4],
            bias_tiles,
            allowed,
            selector,
        )

    grad_queries, grad_tables, unused, grad_keys, grad_values = lax.map(
        back_with_keys, (queries, keys_all, values_all, log_totals, grad_mixed)
    )
    grad_keys, grad_values = (
        lax.psum_scatter(grad_keys, "seq", scatter_dimension=1, tiled=True),
        lax.psum_scatter(grad_values, "seq", scatter_dimension=1, tiled=True),
    )
    grad_table_all = jnp.sum(grad_tables, axis=0)
    grad_projected = jnp.concatenate([grad_queries, grad_keys, grad_values], axis=-1)
    grad_projected = grad_projected.reshape(tokens, 3 * D).astype(jnp.bfloat16)
    grad_w_qkv = jnp.einsum(
        "td,tk->dk", normed_one, grad_projected, preferred_element_type=jnp.float32
    )
    grad_normed_one = jnp.einsum(
        "tk,dk->td", grad_projected, w_qkv, preferred_element_type=jnp.float32
    )
    grad_start_norm, grad_gain_one, grad_shift_one = norm_back_one(grad_normed_one)
    grad_start = grad_middle + grad_start_norm
    grad_embed_local = jnp.einsum(
        "tv,td->vd", picker.astype(jnp.float32), grad_start, precision=lax.Precision.HIGHEST
    )
    local_grads = (
        grad_embed_local.reshape(-1),
        grad_w_qkv.reshape(-1),
        grad_w_out.reshape(-1),
        grad_w_up.reshape(-1),
        grad_w_down.reshape(-1),
        jnp.stack([grad_gain_one, grad_gain_two]).reshape(-1),
        jnp.stack([grad_shift_one, grad_shift_two]).reshape(-1),
        jnp.stack([grad_shift_out, grad_shift_down]).reshape(-1),
        grad_bias_up,
        grad_table_all.reshape(-1),
    )
    summed = (
        lax.psum_scatter(local_grads[0], ("dp", "seq"), scatter_dimension=0, tiled=True),
        lax.psum_scatter(local_grads[1], ("dp", "seq"), scatter_dimension=0, tiled=True),
        lax.psum_scatter(local_grads[2], ("dp", "seq"), scatter_dimension=0, tiled=True),
        lax.psum_scatter(local_grads[3], ("dp", "seq"), scatter_dimension=0, tiled=True),
        lax.psum_scatter(local_grads[4], ("dp", "seq"), scatter_dimension=0, tiled=True),
        lax.psum_scatter(local_grads[5], ("dp", "seq"), scatter_dimension=0, tiled=True),
        lax.psum_scatter(local_grads[6], ("dp", "seq"), scatter_dimension=0, tiled=True),
        lax.psum_scatter(local_grads[7], ("dp", "seq"), scatter_dimension=0, tiled=True),
        lax.psum_scatter(local_grads[8], ("dp", "seq"), scatter_dimension=0, tiled=True),
        lax.psum_scatter(local_grads[9], ("dp", "seq"), scatter_dimension=0, tiled=True),
    )
    return (
        result.reshape(seq_count, local_rows, D).astype(jnp.bfloat16),
        grad_start.reshape(seq_count, local_rows, D).astype(jnp.bfloat16),
        summed[0],
        summed[1],
        summed[2],
        summed[3],
        summed[4],
        summed[5],
        summed[6],
        summed[7],
        summed[8],
        summed[9],
    )


BF16 = jnp.bfloat16
F32 = jnp.float32
ROWS = 128
PAIR = 128
KEYS_AT = (0, 256, 768, 1536)
ROOT_HALF = 0.7071067811865476
ROOT_TAU = 0.3989422804014327


def dot_nn(a, b):
    return jnp.dot(a, b, preferred_element_type=F32)


def dot_nt(a, b):
    return lax.dot_general(a, b, (((1,), (1,)), ((), ())), preferred_element_type=F32)


def dot_tn(a, b):
    return lax.dot_general(a, b, (((0,), (0,)), ((), ())), preferred_element_type=F32)


class Net:
    def __init__(self, send_sems, recv_sems):
        self.send_sems, self.recv_sems, self.copies = send_sems, recv_sems, []

    def send(self, src, dst, device):
        at = len(self.copies)
        copy = pltpu.make_async_remote_copy(
            src_ref=src,
            dst_ref=dst,
            send_sem=self.send_sems.at[at],
            recv_sem=self.recv_sems.at[at],
            device_id=device,
            device_id_type=pl.DeviceIdType.MESH,
        )
        copy.start()
        self.copies.append(copy)
        return copy

    def drain(self):
        for copy in self.copies:
            copy.wait_send()


class Place:
    def __init__(self):
        dp, seq = lax.axis_index("dp"), lax.axis_index("seq")
        self.dp, self.seq = dp, seq
        self.y, self.x = lax.div(dp, 2), lax.rem(dp, 2)
        self.z, self.c = lax.div(seq, 2), lax.rem(seq, 2)
        self.flat = dp * 8 + seq

    def dev(self, y, x, z, c):
        return (y * 2 + x, z * 2 + c)

    def sibling(self):
        return self.dev(self.y, self.x, self.z, 1 - self.c)

    def across_x(self):
        return self.dev(self.y, 1 - self.x, self.z, self.c)

    def across_y(self):
        return self.dev(1 - self.y, self.x, self.z, self.c)

    def ahead(self, step):
        return lax.rem(self.z + step, 4)

    def behind(self, step):
        return lax.rem(self.z + (4 - step), 4)

    def along_z(self, step):
        return self.dev(self.y, self.x, self.ahead(step), self.c)


class Gather:
    def __init__(self, net, at, full, sources=None):
        self.net, self.at, self.full, self.sources = net, at, full, sources

    def along_z(self):
        at = self.at
        own = self.full.at[at.y, at.x, at.z, at.c]
        self.waits = []
        for step in (1, 2, 3):
            src = own if self.sources is None else self.sources.at[at.ahead(step)]
            self.waits.append(self.net.send(src, own, at.along_z(step)))

    def arrive(self):
        for copy in self.waits:
            copy.wait_recv()

    def first(self):
        self.arrive()
        at, full = self.at, self.full
        low = full.at[at.y, at.x, 0:2, at.c]
        high = full.at[at.y, at.x, 2:4, at.c]
        self.waits = [
            self.net.send(low, low, at.across_x()),
            self.net.send(high, high, at.across_y()),
        ]

    def second(self):
        self.arrive()
        at, full = self.at, self.full
        low = full.at[at.y, :, 0:2, at.c]
        high = full.at[:, at.x, 2:4, at.c]
        self.waits = [
            self.net.send(low, low, at.across_y()),
            self.net.send(high, high, at.across_x()),
        ]

    def cores(self):
        self.arrive()
        half = self.full.at[:, :, :, self.at.c]
        self.waits = [self.net.send(half, half, self.at.sibling())]


class Scatter:
    def __init__(self, net, at, part, bufs):
        self.net, self.at, self.part = net, at, part
        self.sums, self.low1, self.high1, self.low2, self.high2, self.last = bufs

    def arrive(self):
        for copy in self.waits:
            copy.wait_recv()

    def cores(self):
        at = self.at
        self.waits = [self.net.send(self.part.at[:, :, :, 1 - at.c], self.sums, at.sibling())]

    def first(self):
        self.arrive()
        at, sums, part = self.at, self.sums, self.part

        def add(i, carry):
            y, x, z = lax.div(i, 8), lax.rem(lax.div(i, 4), 2), lax.rem(i, 4)
            sums[y, x, z] = sums[y, x, z] + part[y, x, z, at.c]
            return carry

        lax.fori_loop(0, 16, add, 0)
        self.waits = [
            self.net.send(sums.at[:, 1 - at.x, 0:2], self.low1, at.across_x()),
            self.net.send(sums.at[1 - at.y, :, 2:4], self.high1, at.across_y()),
        ]

    def second(self):
        self.arrive()
        at, sums = self.at, self.sums

        def add(i, carry):
            a, b = lax.div(i, 2), lax.rem(i, 2)
            sums[a, at.x, b] = sums[a, at.x, b] + self.low1[a, b]
            sums[at.y, a, b + 2] = sums[at.y, a, b + 2] + self.high1[a, b]
            return carry

        lax.fori_loop(0, 4, add, 0)
        self.waits = [
            self.net.send(sums.at[1 - at.y, at.x, 0:2], self.low2, at.across_y()),
            self.net.send(sums.at[at.y, 1 - at.x, 2:4], self.high2, at.across_x()),
        ]

    def along_z(self):
        self.arrive()
        at, sums = self.at, self.sums
        for b in range(2):
            sums[at.y, at.x, b] = sums[at.y, at.x, b] + self.low2[b]
            sums[at.y, at.x, b + 2] = sums[at.y, at.x, b + 2] + self.high2[b]
        self.waits = [
            self.net.send(sums.at[at.y, at.x, at.ahead(s)], self.last.at[s - 1], at.along_z(s))
            for s in (1, 2, 3)
        ]

    def total(self):
        self.arrive()
        at = self.at
        total = self.sums[at.y, at.x, at.z].astype(F32)
        for i in range(3):
            total = total + self.last[i].astype(F32)
        return total


def spread(ref, value, width):
    for j in range(width):
        ref[pl.ds(j, value.shape[0], stride=width), :] = value[:, 128 * j : 128 * j + 128]


def norm_parts(hidden):
    centered = hidden - jnp.mean(hidden, axis=-1, keepdims=True)
    spread_of = jnp.mean(centered * centered, axis=-1, keepdims=True)
    inverse = lax.rsqrt(spread_of + EPSILON)
    return centered * inverse, inverse


def norm_back(upstream, gain_row, normal, inverse):
    scaled = upstream * gain_row
    return inverse * (
        scaled
        - jnp.mean(scaled, axis=-1, keepdims=True)
        - normal * jnp.mean(scaled * normal, axis=-1, keepdims=True)
    )


def column_sum(value):
    return jnp.sum(value, axis=0, keepdims=True)


SHARDS = dict(emb=(32, 128), qkv=(16, 384), out=(16, 512), up=(16, 2048), down=(64, 512))


def scratch():
    vm = pltpu.VMEM
    s = dict(
        lin32=vm((256, 128), F32),
        emb32=vm((1024, 128), F32),
        qkv_src=vm((4, 16, 384), BF16),
        small_w=vm((2, 2, 4, 2, 8, 128), F32),
        small32=vm((256, 128), F32),
        vecs=vm((16, 512), F32),
        rel_row=vm((1, 256), F32),
        bias_row=vm((1, 2048), F32),
        picks=vm((256, 128), BF16),
        start=vm((128, 512), F32),
        normal1=vm((128, 512), F32),
        inverse1=vm((128, 1), F32),
        normed1=vm((4, 128, 512), BF16),
        query=vm((4, 128, 128), BF16),
        keyval=vm((2, 4, 2, 128, 128), BF16),
        probs=vm((2, 128, 2560), F32),
        mixed_out=vm((4, 128, 128), BF16),
        mixed=vm((128, 512), BF16),
        middle=vm((128, 512), F32),
        normal2=vm((128, 512), F32),
        inverse2=vm((128, 1), F32),
        normed2=vm((128, 512), BF16),
        acc1=vm((128, 512), F32),
        acc2=vm((128, 512), F32),
        gub=vm((1, 2048), F32),
        grad_mid=vm((128, 512), F32),
        gmix_src=vm((128, 512), BF16),
        gmix=vm((4, 128, 128), BF16),
        dkv=vm((2, 4, 2, 128, 128), F32),
        dkv_in=vm((2, 4, 128, 128), F32),
        dquery=vm((4, 128, 128), BF16),
        dproj=vm((4, 128, 384), BF16),
        gnorm=vm((4, 128, 512), BF16),
        gnorm_in=vm((3, 128, 512), BF16),
        sg=vm((16, 512), F32),
        sg_in=vm((6, 16, 512), F32),
        gathered=vm((4, 16, 384), BF16),
        small_z=vm((3, 16, 512), F32),
        sg_total=vm((16, 512), F32),
    )
    for name, shard in SHARDS.items():
        s["w_" + name] = vm((2, 2, 4, 2) + shard, BF16)
        s["g_" + name] = vm((2, 2, 4, 2) + shard, BF16)
        s["r0_" + name] = vm((2, 2, 4) + shard, BF16)
        s["r1_" + name] = vm((2, 2) + shard, BF16)
        s["r2_" + name] = vm((2, 2) + shard, BF16)
        s["r3_" + name] = vm((2,) + shard, BF16)
        s["r4_" + name] = vm((2,) + shard, BF16)
        s["r5_" + name] = vm((3,) + shard, BF16)
    s["send_sems"] = pltpu.SemaphoreType.DMA((160,))
    s["recv_sems"] = pltpu.SemaphoreType.DMA((160,))
    return s


INPUTS = ["stream", "ids", "cot", "emb", "qkv", "out", "up", "down", "small"]
OUTPUTS = ["act", "gstream", "o_emb", "o_qkv", "o_out", "o_up", "o_down", "o_small"]


def fused_kernel(*refs):
    names = INPUTS + OUTPUTS + list(scratch())
    v = types.SimpleNamespace(**dict(zip(names, refs, strict=True)))
    at = Place()
    net = Net(v.send_sems, v.recv_sems)
    y, x, z, c = at.y, at.x, at.z, at.c

    barrier = pltpu.get_barrier_semaphore()
    peers = [at.sibling(), at.across_x(), at.across_y()] + [at.along_z(s) for s in (1, 2, 3)]
    for peer in peers:
        pl.semaphore_signal(
            barrier, inc=1, device_id=peer, device_id_type=pl.DeviceIdType.MESH
        )

    v.w_emb[y, x, z, c] = v.emb[...]
    v.small_w[y, x, z, c] = v.small[...]
    v.lin32[0:192, :] = v.qkv[...].astype(F32)
    for t in range(3):
        for zz in range(4):
            piece = v.lin32[pl.ds(4 * t + zz, 16, stride=12), :].astype(BF16)
            v.qkv_src[zz, :, 128 * t : 128 * t + 128] = piece
    v.w_qkv[y, x, z, c] = v.qkv_src[z]
    v.lin32[0:64, :] = v.out[...].astype(F32)
    for j in range(4):
        v.w_out[y, x, z, c, :, 128 * j : 128 * j + 128] = v.lin32[
            pl.ds(j, 16, stride=4), :
        ].astype(BF16)
    v.lin32[...] = v.up[...].astype(F32)
    for j in range(16):
        v.w_up[y, x, z, c, :, 128 * j : 128 * j + 128] = v.lin32[
            pl.ds(j, 16, stride=16), :
        ].astype(BF16)
    v.lin32[...] = v.down[...].astype(F32)
    for j in range(4):
        v.w_down[y, x, z, c, :, 128 * j : 128 * j + 128] = v.lin32[
            pl.ds(j, 64, stride=4), :
        ].astype(BF16)
    pl.semaphore_wait(barrier, len(peers))

    emb = Gather(net, at, v.w_emb)
    small = Gather(net, at, v.small_w)
    qkv = Gather(net, at, v.w_qkv, v.qkv_src)
    out = Gather(net, at, v.w_out)
    up = Gather(net, at, v.w_up)
    down = Gather(net, at, v.w_down)
    fast, slow = (emb, small, qkv), (out, up, down)
    for g in fast:
        g.along_z()
    for g in slow:
        g.along_z()
    for g in fast:
        g.first()
    for g in fast:
        g.second()
    v.picks[...] = (
        (lax.broadcasted_iota(jnp.int32, (VOCAB, ROWS), 0) == v.ids[...]).astype(F32).astype(BF16)
    )
    for g in fast:
        g.cores()
    emb.arrive()
    small.arrive()

    v.small32[...] = v.small_w[...].reshape(256, 128)
    lane = lax.broadcasted_iota(jnp.int32, (128, 512), 1)
    row = lax.broadcasted_iota(jnp.int32, (128, 512), 0)
    owner = lax.broadcasted_iota(jnp.int32, (32, 512), 0)
    where = lax.broadcasted_iota(jnp.int32, (32, 512), 1)

    def tiled(kind, size):
        pieces = v.small32[pl.ds(kind, 32, stride=8), :].astype(BF16)
        select = (lax.rem(lane, size) == row).astype(F32).astype(BF16)
        return dot_nn(pieces, select)

    def picked(wide, size, first):
        return column_sum(jnp.where(owner == first + lax.div(where, size), wide, 0.0))

    for kind in range(3):
        wide = tiled(kind, 32)
        for half in range(2):
            v.vecs[2 * kind + half : 2 * kind + half + 1, :] = picked(wide, 32, 16 * half)
    wide = tiled(3, 64)
    for block in range(4):
        v.bias_row[:, 512 * block : 512 * block + 512] = picked(wide, 64, 8 * block)
    rel_row = picked(tiled(4, 8), 8, 0)[:, 0:256]
    rel_lane = lax.broadcasted_iota(jnp.int32, (1, 256), 1)

    v.emb32[...] = v.w_emb[...].reshape(1024, 128).astype(F32)
    for j in range(4):
        cut = slice(128 * j, 128 * j + 128)
        table = v.emb32[pl.ds(j, VOCAB, stride=4), :].astype(BF16)
        v.start[:, cut] = v.stream[:, cut].astype(F32) + dot_tn(v.picks[...], table)
    normal, inverse = norm_parts(v.start[...])
    v.normal1[...] = normal
    v.inverse1[...] = inverse
    v.normed1[z] = (normal * v.vecs[0:1, :] + v.vecs[2:3, :]).astype(BF16)
    normed_moves = [None] + [
        net.send(v.normed1.at[z], v.normed1.at[z], at.along_z(s)) for s in (1, 2, 3)
    ]

    for g in slow:
        g.first()

    qkv.arrive()
    weight = v.w_qkv[...].reshape(512, 384)
    moves = []
    for s in range(4):
        if s:
            normed_moves[s].wait_recv()
        zs = at.behind(s)
        projected = dot_nn(v.normed1[zs], weight).astype(BF16)
        v.query[zs] = projected[:, 0:128]
        v.keyval[0, zs, c] = projected[:, 128:256]
        v.keyval[1, zs, c] = projected[:, 256:384]
        both = v.keyval.at[:, zs, c]
        moves.append(net.send(both, both, at.sibling()))
        if s == 1:
            for g in slow:
                g.second()
    for copy in moves:
        copy.wait_recv()

    pair_lane = lax.broadcasted_iota(jnp.int32, (ROWS, PAIR), 1)
    head_lanes = (pair_lane < HEAD_DIM, pair_lane >= HEAD_DIM)

    def rel_value(head, distance):
        spot = (2 * z + head) * BUCKETS + distance
        return jnp.sum(jnp.where(rel_lane == spot, rel_row, 0.0), axis=1, keepdims=True)

    rel_values = [[rel_value(h, d) for d in range(4)] for h in range(2)]
    zero = jnp.zeros((), BF16)
    for zq in range(4):
        count = 256 * (zq + 1)
        keys = v.keyval[0, 0 : zq + 1].reshape(count, PAIR)
        vals = v.keyval[1, 0 : zq + 1].reshape(count, PAIR)
        heads = []
        for h in range(2):
            query = jnp.where(head_lanes[h], v.query[zq], zero)
            bias = jnp.concatenate(
                [
                    jnp.broadcast_to(rel_values[h][zq - zk], (1, 256))
                    for zk in range(zq + 1)
                ],
                axis=1,
            )
            scores = dot_nt(query, keys) * SCALING + bias
            shifted = jnp.exp(scores - jnp.max(scores, axis=-1, keepdims=True))
            probs = shifted / jnp.sum(shifted, axis=-1, keepdims=True)
            v.probs[h, :, KEYS_AT[zq] : KEYS_AT[zq] + count] = probs
            heads.append(dot_nn(probs.astype(BF16), vals))
        v.mixed_out[zq] = jnp.where(head_lanes[0], heads[0], heads[1]).astype(BF16)
    own_lanes = pl.ds(pl.multiple_of(z * PAIR, PAIR), PAIR)
    moves = [
        net.send(v.mixed_out.at[at.ahead(s)], v.mixed.at[:, own_lanes], at.along_z(s))
        for s in (1, 2, 3)
    ]
    v.mixed[:, own_lanes] = v.mixed_out[z]
    for g in slow:
        g.cores()
    for copy in moves:
        copy.wait_recv()

    out.arrive()
    mixed = v.mixed[...]
    out_weight = v.w_out[...].reshape(512, 512)
    middle = v.start[...] + dot_nn(mixed, out_weight) + v.vecs[4:5, :]
    v.middle[...] = middle
    normal, inverse = norm_parts(middle)
    v.normal2[...] = normal
    v.inverse2[...] = inverse
    v.normed2[...] = (normal * v.vecs[1:2, :] + v.vecs[3:4, :]).astype(BF16)
    v.acc1[...] = jnp.zeros_like(v.acc1)
    v.acc2[...] = jnp.zeros_like(v.acc2)
    up.arrive()
    down.arrive()

    def hidden_tile(i, carry):
        cols = pl.ds(pl.multiple_of(i * 256, 256), 256)
        ty, tx, tz = lax.div(i, 4), lax.rem(lax.div(i, 2), 2), lax.rem(i, 2) * 2
        normed = v.normed2[...]
        grad = v.cot[...]
        up_tile = v.w_up[:, :, :, :, :, cols].reshape(512, 256)
        down_tile = v.w_down[ty, tx, pl.ds(tz, 2)].reshape(256, 512)
        lifted = dot_nn(normed, up_tile) + v.bias_row[:, cols]
        share = 0.5 * (1.0 + lax.erf(lifted * ROOT_HALF))
        active = (lifted * share).astype(BF16)
        slope = share + lifted * (jnp.exp(-0.5 * lifted * lifted) * ROOT_TAU)
        v.acc1[...] += dot_nn(active, down_tile)
        grad_lifted = dot_nt(grad, down_tile) * slope
        v.gub[:, cols] = column_sum(grad_lifted)
        low = grad_lifted.astype(BF16)
        v.acc2[...] += dot_nt(low, up_tile)
        v.g_down[ty, tx, pl.ds(tz, 2)] = dot_tn(active, grad).astype(BF16).reshape(2, 2, 64, 512)
        v.g_up[:, :, :, :, :, cols] = dot_tn(normed, low).astype(BF16).reshape(2, 2, 4, 2, 16, 256)
        return carry

    lax.fori_loop(0, 8, hidden_tile, 0)

    def scatter(name):
        bufs = [getattr(v, f"r{i}_{name}") for i in range(6)]
        return Scatter(net, at, getattr(v, "g_" + name), bufs)

    s_down, s_up, s_out, s_qkv, s_emb = (
        scatter(n) for n in ("down", "up", "out", "qkv", "emb")
    )
    s_down.cores()
    s_up.cores()
    grad_wide = v.cot[...].astype(F32)
    v.act[...] = (v.middle[...] + v.acc1[...] + v.vecs[5:6, :]).astype(BF16)
    upstream = v.acc2[...]
    normal = v.normal2[...]
    v.sg[1:2, :] = column_sum(upstream * normal)
    v.sg[3:4, :] = column_sum(upstream)
    v.sg[5:6, :] = column_sum(grad_wide)
    grad_middle = grad_wide + norm_back(upstream, v.vecs[1:2, :], normal, v.inverse2[...])
    v.grad_mid[...] = grad_middle
    v.sg[4:5, :] = column_sum(grad_middle)
    for block in range(4):
        v.sg[6 + block : 7 + block, :] = v.gub[:, 512 * block : 512 * block + 512]
    middle_low = grad_middle.astype(BF16)
    v.gmix_src[...] = dot_nt(middle_low, v.w_out[...].reshape(512, 512)).astype(BF16)
    moves = [
        net.send(
            v.gmix_src.at[:, pl.ds(pl.multiple_of(at.ahead(s) * PAIR, PAIR), PAIR)],
            v.gmix.at[z],
            at.along_z(s),
        )
        for s in (1, 2, 3)
    ]
    v.gmix[z] = v.gmix_src[:, own_lanes]
    v.g_out[...] = dot_tn(v.mixed[...], middle_low).astype(BF16).reshape(2, 2, 4, 2, 16, 512)
    s_out.cores()
    s_down.first()
    s_up.first()
    s_out.first()
    for copy in moves:
        copy.wait_recv()

    rel_sums = [[jnp.zeros((1, 256), F32) for d in range(4)] for h in range(2)]
    core_moves = {}
    for zq in (3, 2, 1, 0):
        count = 256 * (zq + 1)
        keys = v.keyval[0, 0 : zq + 1].reshape(count, PAIR)
        vals = v.keyval[1, 0 : zq + 1].reshape(count, PAIR)
        heads, dkeys, dvals = [], 0.0, 0.0
        for h in range(2):
            query = jnp.where(head_lanes[h], v.query[zq], zero)
            grad = jnp.where(head_lanes[h], v.gmix[zq], zero)
            probs = v.probs[h, :, KEYS_AT[zq] : KEYS_AT[zq] + count]
            grad_probs = dot_nt(grad, vals)
            inner = jnp.sum(probs * grad_probs, axis=-1, keepdims=True)
            grad_scores = probs * (grad_probs - inner)
            for zk in range(zq + 1):
                tile = grad_scores[:, 256 * zk : 256 * zk + 256]
                rel_sums[h][zq - zk] = rel_sums[h][zq - zk] + column_sum(tile)
            low = grad_scores.astype(BF16)
            heads.append(dot_nn(low, keys))
            dkeys = dkeys + dot_tn(low, query)
            dvals = dvals + dot_tn(probs.astype(BF16), grad)
        v.dquery[zq] = (jnp.where(head_lanes[0], heads[0], heads[1]) * SCALING).astype(BF16)
        dkeys = dkeys.reshape(zq + 1, 2, ROWS, PAIR)
        dvals = dvals.reshape(zq + 1, 2, ROWS, PAIR)
        if zq == 3:
            v.dkv[0] = dkeys
            v.dkv[1] = dvals
        else:
            v.dkv[0, 0 : zq + 1] += dkeys
            v.dkv[1, 0 : zq + 1] += dvals
        core_moves[zq] = net.send(
            v.dkv.at[:, zq, 1 - c], v.dkv_in.at[:, zq], at.sibling()
        )
        if zq == 2:
            s_down.second()
            s_up.second()
            s_out.second()
    weight = v.w_qkv[...].reshape(512, 384)
    for zq in (3, 2, 1, 0):
        core_moves[zq].wait_recv()
        dkeys = (v.dkv[0, zq, c] + v.dkv_in[0, zq]) * SCALING
        dvals = v.dkv[1, zq, c] + v.dkv_in[1, zq]
        v.dproj[zq, :, 0:128] = v.dquery[zq]
        v.dproj[zq, :, 128:256] = dkeys.astype(BF16)
        v.dproj[zq, :, 256:384] = dvals.astype(BF16)
        v.gnorm[zq] = dot_nt(v.dproj[zq], weight).astype(BF16)
    gnorm_moves = [
        net.send(v.gnorm.at[at.ahead(s)], v.gnorm_in.at[s - 1], at.along_z(s)) for s in (1, 2, 3)
    ]
    v.g_qkv[...] = (
        dot_tn(v.normed1[...].reshape(512, 512), v.dproj[...].reshape(512, 384))
        .astype(BF16)
        .reshape(2, 2, 4, 2, 16, 384)
    )
    s_qkv.cores()
    s_down.along_z()
    s_up.along_z()
    s_out.along_z()
    s_qkv.first()
    sums = jnp.zeros((1, 512), F32)
    wide_lane = lax.broadcasted_iota(jnp.int32, (1, 512), 1)
    for h in range(2):
        for d in range(4):
            spot = (2 * z + h) * BUCKETS + d
            value = jnp.sum(rel_sums[h][d], axis=1, keepdims=True)
            sums = sums + jnp.where(wide_lane == spot, value, 0.0)
    v.sg[10:11, :] = sums
    v.sg[11:16, :] = jnp.zeros((5, 512), F32)

    upstream = v.gnorm[z].astype(F32)
    for s in range(3):
        gnorm_moves[s].wait_recv()
        upstream = upstream + v.gnorm_in[s].astype(F32)
    normal = v.normal1[...]
    v.sg[0:1, :] = column_sum(upstream * normal)
    v.sg[2:3, :] = column_sum(upstream)
    grad_start = v.grad_mid[...] + norm_back(upstream, v.vecs[0:1, :], normal, v.inverse1[...])
    start_low = grad_start.astype(BF16)
    small_move = net.send(v.sg, v.sg_in.at[0], at.sibling())
    grad_embed = dot_nn(v.picks[...], start_low)
    spread(v.emb32, grad_embed, 4)
    v.g_emb[...] = v.emb32[...].astype(BF16).reshape(2, 2, 4, 2, 32, 128)
    s_emb.cores()
    v.gstream[...] = start_low
    s_qkv.second()
    small_move.wait_recv()
    v.sg_in[4] = v.sg[...] + v.sg_in[0]
    small_move = net.send(v.sg_in.at[4], v.sg_in.at[1], at.across_x())
    s_emb.first()
    spread(v.o_down, s_down.total(), 4)
    small_move.wait_recv()
    v.sg_in[5] = v.sg_in[4] + v.sg_in[1]
    small_move = net.send(v.sg_in.at[5], v.sg_in.at[2], at.across_y())
    s_qkv.along_z()
    s_emb.second()
    spread(v.o_up, s_up.total(), 16)
    small_move.wait_recv()
    total = v.sg_in[5] + v.sg_in[2]
    v.sg_in[3] = total
    small_moves = [
        net.send(v.sg_in.at[3], v.small_z.at[s - 1], at.along_z(s)) for s in (1, 2, 3)
    ]
    s_emb.along_z()
    spread(v.o_out, s_out.total(), 4)
    s_qkv.arrive()
    v.gathered[z] = v.r0_qkv[y, x, z]
    for s in (1, 2, 3):
        v.gathered[at.behind(s)] = v.r5_qkv[s - 1]
    for zz in range(4):
        piece = v.gathered[zz].astype(F32)
        for t in range(3):
            v.o_qkv[pl.ds(4 * t + zz, 16, stride=12), :] = piece[:, 128 * t : 128 * t + 128]
    for s in range(3):
        small_moves[s].wait_recv()
        total = total + v.small_z[s]
    v.sg_total[...] = total

    def shard(row_at, offset):
        line = jnp.broadcast_to(v.sg_total[pl.ds(row_at, 1), :], (8, 512))
        return pltpu.roll(line, lax.rem(512 - offset, 512), 1)[0:1, 0:128]

    line = 32 * lax.rem(at.flat, 16)
    v.o_small[0:1, :] = shard(y, line)
    v.o_small[1:2, :] = shard(2 + y, line)
    v.o_small[2:3, :] = shard(4 + y, line)
    v.o_small[3:4, :] = shard(6 + at.dp, 64 * at.seq)
    v.o_small[4:5, :] = shard(10, 8 * at.flat)
    v.o_small[5:8, :] = jnp.zeros((3, 128), F32)
    v.o_emb[...] = s_emb.total()
    net.drain()


def fused_local(
    stream,
    byte_ids,
    cotangent,
    embed_flat,
    qkv_flat,
    out_flat,
    up_flat,
    down_flat,
    gains,
    norm_shifts,
    out_shifts,
    up_bias,
    rel_bias,
):
    def line(piece):
        return jnp.pad(piece.astype(F32), (0, 128 - piece.shape[0]))[None]

    small = jnp.concatenate(
        [line(p) for p in (gains, norm_shifts, out_shifts, up_bias, rel_bias)]
        + [jnp.zeros((3, 128), F32)]
    )
    operands = (
        stream.reshape(ROWS, D),
        byte_ids,
        cotangent.reshape(ROWS, D),
        embed_flat.reshape(-1, 128),
        qkv_flat.reshape(-1, 128),
        out_flat.reshape(-1, 128),
        up_flat.reshape(-1, 128),
        down_flat.reshape(-1, 128),
        small,
    )
    shapes = (
        ((ROWS, D), BF16),
        ((ROWS, D), BF16),
        ((32, 128), F32),
        ((192, 128), F32),
        ((64, 128), F32),
        ((256, 128), F32),
        ((256, 128), F32),
        ((8, 128), F32),
    )
    whole = pl.BlockSpec(memory_space=pltpu.VMEM)
    act, gstream, g_emb, g_qkv, g_out, g_up, g_down, g_small = pl.pallas_call(
        fused_kernel,
        out_shape=[jax.ShapeDtypeStruct(s, t) for s, t in shapes],
        in_specs=[whole] * len(operands),
        out_specs=[whole] * len(shapes),
        scratch_shapes=list(scratch().values()),
        compiler_params=pltpu.CompilerParams(
            collective_id=0, has_side_effects=True, vmem_limit_bytes=60 << 20
        ),
        name="layer",
    )(*operands)
    return (
        act.reshape(stream.shape),
        gstream.reshape(stream.shape),
        g_emb.reshape(-1),
        g_qkv.reshape(-1),
        g_out.reshape(-1),
        g_up.reshape(-1),
        g_down.reshape(-1),
        g_small[0, : gains.shape[0]],
        g_small[1, : norm_shifts.shape[0]],
        g_small[2, : out_shifts.shape[0]],
        g_small[3, : up_bias.shape[0]],
        g_small[4, : rel_bias.shape[0]],
    )


def solution(mesh):
    body = fused_local if (mesh.shape["dp"], mesh.shape["seq"]) == (4, 8) else local
    in_specs = (
        P("dp", "seq", None),
        P("dp", "seq"),
        P("dp", "seq", None),
        P(("dp", "seq")),
        P(("dp", "seq")),
        P(("dp", "seq")),
        P(("dp", "seq")),
        P(("dp", "seq")),
        P(("dp", "seq")),
        P(("dp", "seq")),
        P(("dp", "seq")),
        P(("dp", "seq")),
        P(("dp", "seq")),
    )
    out_specs = (
        P("dp", "seq", None),
        P("dp", "seq", None),
        P(("dp", "seq")),
        P(("dp", "seq")),
        P(("dp", "seq")),
        P(("dp", "seq")),
        P(("dp", "seq")),
        P(("dp", "seq")),
        P(("dp", "seq")),
        P(("dp", "seq")),
        P(("dp", "seq")),
        P(("dp", "seq")),
    )
    return jax.shard_map(body, mesh=mesh, in_specs=in_specs, out_specs=out_specs, check_vma=False)
```

```python
import types

import jax
import jax.numpy as jnp
from jax import lax
from jax.experimental import pallas as pl
from jax.experimental.pallas import tpu as pltpu
from jax.sharding import PartitionSpec as P

D = 512
HEADS = 8
HEAD_DIM = 64
FF = 2048
VOCAB = 256
BLOCK = 256
BUCKETS = 32


EPSILON = 1e-05
SCALING = 0.125
MASKED = -1e30


def layer_norm(hidden, gain_row, shift_row):
    centered = hidden - jnp.mean(hidden, axis=-1, keepdims=True)
    spread = jnp.mean(centered * centered, axis=-1, keepdims=True)
    return centered * lax.rsqrt(spread + EPSILON) * gain_row + shift_row


def gelu_exact(values):
    return jax.nn.gelu(values, approximate=False)


def unpack(gathered):
    embed, w_qkv, w_out, w_up, w_down, gain_flat, norm_flat, out_flat, bias_flat, rel_flat = (
        gathered
    )
    return (
        embed.reshape(VOCAB, D),
        w_qkv.reshape(D, 3 * D),
        w_out.reshape(D, D),
        w_up.reshape(D, FF),
        w_down.reshape(FF, D),
        gain_flat.astype(jnp.float32).reshape(2, D),
        norm_flat.astype(jnp.float32).reshape(2, D),
        out_flat.astype(jnp.float32).reshape(2, D),
        bias_flat.astype(jnp.float32),
        rel_flat.astype(jnp.float32).reshape(HEADS, BUCKETS),
    )


def block_terms(rel_table, row_first, row_count, key_first, key_count):
    row_blocks = max(row_count // BLOCK, 1)
    key_blocks = max(key_count // BLOCK, 1)
    row_ids = row_first // BLOCK + jnp.arange(row_blocks, dtype=jnp.int32)
    key_ids = key_first // BLOCK + jnp.arange(key_blocks, dtype=jnp.int32)
    distance = row_ids[:, None] - key_ids[None, :]
    allowed = distance >= 0
    bucket = jnp.clip(distance, 0, BUCKETS - 1)
    selector = (bucket[:, :, None] == jnp.arange(BUCKETS, dtype=jnp.int32)[None, None, :]).astype(
        jnp.float32
    )
    bias_tiles = jnp.einsum("abn,hn->hab", selector, rel_table, precision=lax.Precision.HIGHEST)
    return (bias_tiles, allowed, selector)


def score_tile(query_heads, key_heads, bias_tiles, allowed):
    row_count = query_heads.shape[0]
    key_count = key_heads.shape[0]
    raw_scores = (
        jnp.einsum("qhd,khd->hqk", query_heads, key_heads, preferred_element_type=jnp.float32)
        * SCALING
    )
    row_blocks = bias_tiles.shape[1]
    key_blocks = bias_tiles.shape[2]
    tiled = raw_scores.reshape(
        HEADS, row_blocks, row_count // row_blocks, key_blocks, key_count // key_blocks
    )
    tiled = tiled + bias_tiles[:, :, None, :, None]
    tiled = jnp.where(allowed[None, :, None, :, None], tiled, MASKED)
    return tiled.reshape(HEADS, row_count, key_count)


def heads_of(rows):
    return rows.reshape(rows.shape[0], HEADS, HEAD_DIM)


def attend(queries, key_rows, value_rows, bias_tiles, allowed):
    local_rows = queries.shape[0]
    scores = score_tile(heads_of(queries), heads_of(key_rows), bias_tiles, allowed)
    row_max = jnp.max(scores, axis=-1, keepdims=True)
    shifted = jnp.exp(scores - row_max)
    row_sum = jnp.sum(shifted, axis=-1, keepdims=True)
    soft_weights = (shifted / row_sum).astype(jnp.bfloat16)
    mixed_heads = jnp.einsum(
        "hqk,khd->qhd", soft_weights, heads_of(value_rows), preferred_element_type=jnp.float32
    )
    return (mixed_heads.reshape(local_rows, D), (row_max + jnp.log(row_sum))[:, :, 0])


def row_back(queries, key_rows, value_rows, log_totals, grad_mixed, bias_tiles, allowed, selector):
    local_rows = queries.shape[0]
    seq_length = key_rows.shape[0]
    query_heads = heads_of(queries)
    key_heads = heads_of(key_rows)
    value_heads = heads_of(value_rows)
    grad_heads = heads_of(grad_mixed)
    scores = score_tile(query_heads, key_heads, bias_tiles, allowed)
    soft_weights = jnp.exp(scores - log_totals[:, :, None])
    grad_weights = jnp.einsum(
        "qhd,khd->hqk", grad_heads, value_heads, preferred_element_type=jnp.float32
    )
    row_inner = jnp.sum(soft_weights * grad_weights, axis=-1)
    grad_scores = soft_weights * (grad_weights - row_inner[:, :, None])
    row_blocks = bias_tiles.shape[1]
    key_blocks = bias_tiles.shape[2]
    tile_sums = jnp.sum(
        grad_scores.reshape(
            HEADS, row_blocks, local_rows // row_blocks, key_blocks, seq_length // key_blocks
        ),
        axis=(2, 4),
    )
    grad_table = jnp.einsum("hab,abn->hn", tile_sums, selector, precision=lax.Precision.HIGHEST)
    scores_low = grad_scores.astype(jnp.bfloat16)
    grad_queries = (
        jnp.einsum("hqk,khd->qhd", scores_low, key_heads, preferred_element_type=jnp.float32)
        * SCALING
    )
    grad_queries = grad_queries.reshape(local_rows, D)
    grad_keys = (
        jnp.einsum("hqk,qhd->khd", scores_low, query_heads, preferred_element_type=jnp.float32)
        * SCALING
    )
    grad_values = jnp.einsum(
        "hqk,qhd->khd",
        soft_weights.astype(jnp.bfloat16),
        grad_heads,
        preferred_element_type=jnp.float32,
    )
    return (
        grad_queries,
        grad_table,
        row_inner,
        grad_keys.reshape(seq_length, D),
        grad_values.reshape(seq_length, D),
    )


def local(
    stream,
    byte_ids,
    cotangent,
    embed_flat,
    qkv_flat,
    out_flat,
    up_flat,
    down_flat,
    gains,
    norm_shifts,
    out_shifts,
    up_bias,
    rel_bias,
):
    seq_count = stream.shape[0]
    local_rows = stream.shape[1]
    seq_length = local_rows * lax.axis_size("seq")
    tokens = seq_count * local_rows
    first_row = lax.axis_index("seq") * local_rows
    owned = (
        embed_flat,
        qkv_flat,
        out_flat,
        up_flat,
        down_flat,
        gains,
        norm_shifts,
        out_shifts,
        up_bias,
        rel_bias,
    )
    gathered = (
        lax.all_gather(owned[0], ("dp", "seq"), axis=0, tiled=True),
        lax.all_gather(owned[1], ("dp", "seq"), axis=0, tiled=True),
        lax.all_gather(owned[2], ("dp", "seq"), axis=0, tiled=True),
        lax.all_gather(owned[3], ("dp", "seq"), axis=0, tiled=True),
        lax.all_gather(owned[4], ("dp", "seq"), axis=0, tiled=True),
        lax.all_gather(owned[5], ("dp", "seq"), axis=0, tiled=True),
        lax.all_gather(owned[6], ("dp", "seq"), axis=0, tiled=True),
        lax.all_gather(owned[7], ("dp", "seq"), axis=0, tiled=True),
        lax.all_gather(owned[8], ("dp", "seq"), axis=0, tiled=True),
        lax.all_gather(owned[9], ("dp", "seq"), axis=0, tiled=True),
    )
    embed, w_qkv, w_out, w_up, w_down, gain_pair, norm_pair, out_pair, bias_up, rel_table = unpack(
        gathered
    )
    picker = byte_ids.reshape(tokens, 1) == jnp.arange(VOCAB, dtype=jnp.int32)[None, :]
    embedded = jnp.dot(picker.astype(jnp.bfloat16), embed, preferred_element_type=jnp.float32)
    start_rows = stream.reshape(tokens, D).astype(jnp.float32) + embedded
    normed_wide, norm_back_one = jax.vjp(layer_norm, start_rows, gain_pair[0], norm_pair[0])
    normed_one = normed_wide.astype(jnp.bfloat16)
    projected = jnp.dot(normed_one, w_qkv, preferred_element_type=jnp.float32).astype(jnp.bfloat16)
    queries = projected[:, :D].reshape(seq_count, local_rows, D)
    key_rows = projected[:, D : 2 * D].reshape(seq_count, local_rows, D)
    value_rows = projected[:, 2 * D :].reshape(seq_count, local_rows, D)
    keys_all, values_all = (
        lax.all_gather(key_rows, "seq", axis=1, tiled=True),
        lax.all_gather(value_rows, "seq", axis=1, tiled=True),
    )
    bias_tiles, allowed, selector = block_terms(rel_table, first_row, local_rows, 0, seq_length)

    def attend_single(operands):
        return attend(operands[0], operands[1], operands[2], bias_tiles, allowed)

    mixed, log_totals = lax.map(attend_single, (queries, keys_all, values_all))
    mixed_low = mixed.reshape(tokens, D).astype(jnp.bfloat16)
    middle = (
        start_rows + jnp.dot(mixed_low, w_out, preferred_element_type=jnp.float32) + out_pair[0]
    )
    normed_mid, norm_back_two = jax.vjp(layer_norm, middle, gain_pair[1], norm_pair[1])
    normed_two = normed_mid.astype(jnp.bfloat16)
    lifted = jnp.dot(normed_two, w_up, preferred_element_type=jnp.float32) + bias_up
    activated, gelu_back = jax.vjp(gelu_exact, lifted)
    active = activated.astype(jnp.bfloat16)
    result = middle + jnp.dot(active, w_down, preferred_element_type=jnp.float32) + out_pair[1]
    gathered_again = (
        lax.all_gather(owned[0], ("dp", "seq"), axis=0, tiled=True),
        lax.all_gather(owned[1], ("dp", "seq"), axis=0, tiled=True),
        lax.all_gather(owned[2], ("dp", "seq"), axis=0, tiled=True),
        lax.all_gather(owned[3], ("dp", "seq"), axis=0, tiled=True),
        lax.all_gather(owned[4], ("dp", "seq"), axis=0, tiled=True),
        lax.all_gather(owned[5], ("dp", "seq"), axis=0, tiled=True),
        lax.all_gather(owned[6], ("dp", "seq"), axis=0, tiled=True),
        lax.all_gather(owned[7], ("dp", "seq"), axis=0, tiled=True),
        lax.all_gather(owned[8], ("dp", "seq"), axis=0, tiled=True),
        lax.all_gather(owned[9], ("dp", "seq"), axis=0, tiled=True),
    )
    embed, w_qkv, w_out, w_up, w_down, gain_pair, norm_pair, out_pair, bias_up, rel_table = unpack(
        gathered_again
    )
    grad_output = cotangent.reshape(tokens, D)
    grad_wide = grad_output.astype(jnp.float32)
    grad_shift_down = jnp.sum(grad_wide, axis=0)
    grad_w_down = jnp.einsum("tf,td->fd", active, grad_output, preferred_element_type=jnp.float32)
    grad_active = jnp.einsum("td,fd->tf", grad_output, w_down, preferred_element_type=jnp.float32)
    (grad_lifted,) = gelu_back(grad_active)
    grad_bias_up = jnp.sum(grad_lifted, axis=0)
    lifted_low = grad_lifted.astype(jnp.bfloat16)
    grad_w_up = jnp.einsum("td,tf->df", normed_two, lifted_low, preferred_element_type=jnp.float32)
    grad_normed_two = jnp.einsum("tf,df->td", lifted_low, w_up, preferred_element_type=jnp.float32)
    grad_mid_norm, grad_gain_two, grad_shift_two = norm_back_two(grad_normed_two)
    grad_middle = grad_wide + grad_mid_norm
    grad_shift_out = jnp.sum(grad_middle, axis=0)
    middle_low = grad_middle.astype(jnp.bfloat16)
    grad_w_out = jnp.einsum("te,td->ed", mixed_low, middle_low, preferred_element_type=jnp.float32)
    grad_mixed = jnp.einsum("td,ed->te", middle_low, w_out, preferred_element_type=jnp.float32)
    grad_mixed = grad_mixed.astype(jnp.bfloat16).reshape(seq_count, local_rows, D)
    keys_all, values_all = (
        lax.all_gather(key_rows, "seq", axis=1, tiled=True),
        lax.all_gather(value_rows, "seq", axis=1, tiled=True),
    )

    def back_with_keys(operands):
        return row_back(
            operands[0],
            operands[1],
            operands[2],
            operands[3],
            operands[4],
            bias_tiles,
            allowed,
            selector,
        )

    grad_queries, grad_tables, unused, grad_keys, grad_values = lax.map(
        back_with_keys, (queries, keys_all, values_all, log_totals, grad_mixed)
    )
    grad_keys, grad_values = (
        lax.psum_scatter(grad_keys, "seq", scatter_dimension=1, tiled=True),
        lax.psum_scatter(grad_values, "seq", scatter_dimension=1, tiled=True),
    )
    grad_table_all = jnp.sum(grad_tables, axis=0)
    grad_projected = jnp.concatenate([grad_queries, grad_keys, grad_values], axis=-1)
    grad_projected = grad_projected.reshape(tokens, 3 * D).astype(jnp.bfloat16)
    grad_w_qkv = jnp.einsum(
        "td,tk->dk", normed_one, grad_projected, preferred_element_type=jnp.float32
    )
    grad_normed_one = jnp.einsum(
        "tk,dk->td", grad_projected, w_qkv, preferred_element_type=jnp.float32
    )
    grad_start_norm, grad_gain_one, grad_shift_one = norm_back_one(grad_normed_one)
    grad_start = grad_middle + grad_start_norm
    grad_embed_local = jnp.einsum(
        "tv,td->vd", picker.astype(jnp.float32), grad_start, precision=lax.Precision.HIGHEST
    )
    local_grads = (
        grad_embed_local.reshape(-1),
        grad_w_qkv.reshape(-1),
        grad_w_out.reshape(-1),
        grad_w_up.reshape(-1),
        grad_w_down.reshape(-1),
        jnp.stack([grad_gain_one, grad_gain_two]).reshape(-1),
        jnp.stack([grad_shift_one, grad_shift_two]).reshape(-1),
        jnp.stack([grad_shift_out, grad_shift_down]).reshape(-1),
        grad_bias_up,
        grad_table_all.reshape(-1),
    )
    summed = (
        lax.psum_scatter(local_grads[0], ("dp", "seq"), scatter_dimension=0, tiled=True),
        lax.psum_scatter(local_grads[1], ("dp", "seq"), scatter_dimension=0, tiled=True),
        lax.psum_scatter(local_grads[2], ("dp", "seq"), scatter_dimension=0, tiled=True),
        lax.psum_scatter(local_grads[3], ("dp", "seq"), scatter_dimension=0, tiled=True),
        lax.psum_scatter(local_grads[4], ("dp", "seq"), scatter_dimension=0, tiled=True),
        lax.psum_scatter(local_grads[5], ("dp", "seq"), scatter_dimension=0, tiled=True),
        lax.psum_scatter(local_grads[6], ("dp", "seq"), scatter_dimension=0, tiled=True),
        lax.psum_scatter(local_grads[7], ("dp", "seq"), scatter_dimension=0, tiled=True),
        lax.psum_scatter(local_grads[8], ("dp", "seq"), scatter_dimension=0, tiled=True),
        lax.psum_scatter(local_grads[9], ("dp", "seq"), scatter_dimension=0, tiled=True),
    )
    return (
        result.reshape(seq_count, local_rows, D).astype(jnp.bfloat16),
        grad_start.reshape(seq_count, local_rows, D).astype(jnp.bfloat16),
        summed[0],
        summed[1],
        summed[2],
        summed[3],
        summed[4],
        summed[5],
        summed[6],
        summed[7],
        summed[8],
        summed[9],
    )


BF16 = jnp.bfloat16
F32 = jnp.float32
ROWS = 128
PAIR = 128
KEYS_AT = (0, 256, 768, 1536)
ROOT_HALF = 0.7071067811865476
ROOT_TAU = 0.3989422804014327


def dot_nn(a, b):
    return jnp.dot(a, b, preferred_element_type=F32)


def dot_nt(a, b):
    return lax.dot_general(a, b, (((1,), (1,)), ((), ())), preferred_element_type=F32)


def dot_tn(a, b):
    return lax.dot_general(a, b, (((0,), (0,)), ((), ())), preferred_element_type=F32)


class Net:
    def __init__(self, send_sems, recv_sems):
        self.send_sems, self.recv_sems, self.copies = send_sems, recv_sems, []

    def send(self, src, dst, device):
        at = len(self.copies)
        copy = pltpu.make_async_remote_copy(
            src_ref=src,
            dst_ref=dst,
            send_sem=self.send_sems.at[at],
            recv_sem=self.recv_sems.at[at],
            device_id=device,
            device_id_type=pl.DeviceIdType.MESH,
        )
        copy.start()
        self.copies.append(copy)
        return copy

    def slots(self, count):
        first = len(self.copies)
        self.copies.extend([None] * count)
        return first

    def copy(self, src, dst, device, send_at, recv_at):
        return pltpu.make_async_remote_copy(
            src_ref=src,
            dst_ref=dst,
            send_sem=self.send_sems.at[send_at],
            recv_sem=self.recv_sems.at[recv_at],
            device_id=device,
            device_id_type=pl.DeviceIdType.MESH,
        )

    def drain(self):
        for copy in self.copies:
            if copy is not None:
                copy.wait_send()


class Place:
    def __init__(self):
        dp, seq = lax.axis_index("dp"), lax.axis_index("seq")
        self.dp, self.seq = dp, seq
        self.y, self.x = lax.div(dp, 2), lax.rem(dp, 2)
        self.z, self.c = lax.div(seq, 2), lax.rem(seq, 2)
        self.flat = dp * 8 + seq

    def dev(self, y, x, z, c):
        return (y * 2 + x, z * 2 + c)

    def sibling(self):
        return self.dev(self.y, self.x, self.z, 1 - self.c)

    def across_x(self):
        return self.dev(self.y, 1 - self.x, self.z, self.c)

    def across_y(self):
        return self.dev(1 - self.y, self.x, self.z, self.c)

    def near(self):
        return self.z + 1 - 2 * lax.rem(self.z, 2)

    def toward(self, z):
        return self.dev(self.y, self.x, z, self.c)

    def others(self):
        return [
            (dy, dx, dz) for dz in (2, 1, 3, 0) for dy in (1, 0) for dx in (1, 0) if dy + dx + dz
        ]

    def other(self, dy, dx, dz):
        y = 1 - self.y if dy else self.y
        x = 1 - self.x if dx else self.x
        return y, x, self.ahead(dz)

    def ahead(self, step):
        return lax.rem(self.z + step, 4)

    def behind(self, step):
        return lax.rem(self.z + (4 - step), 4)

    def along_z(self, step):
        return self.dev(self.y, self.x, self.ahead(step), self.c)


class Gather:
    def __init__(self, net, at, full, sources=None):
        self.net, self.at, self.full, self.sources = net, at, full, sources

    def along_z(self):
        at = self.at
        own = self.full.at[at.y, at.x, at.z, at.c]
        self.waits = []
        for step in (1, 2, 3):
            src = own if self.sources is None else self.sources.at[at.ahead(step)]
            self.waits.append(self.net.send(src, own, at.along_z(step)))

    def arrive(self):
        for copy in self.waits:
            copy.wait_recv()

    def first(self):
        self.arrive()
        at, full = self.at, self.full
        low = full.at[at.y, at.x, 0:2, at.c]
        high = full.at[at.y, at.x, 2:4, at.c]
        self.waits = [
            self.net.send(low, low, at.across_x()),
            self.net.send(high, high, at.across_y()),
        ]

    def second(self):
        self.arrive()
        at, full = self.at, self.full
        low = full.at[at.y, :, 0:2, at.c]
        high = full.at[:, at.x, 2:4, at.c]
        self.waits = [
            self.net.send(low, low, at.across_y()),
            self.net.send(high, high, at.across_x()),
        ]

    def cores(self):
        self.arrive()
        half = self.full.at[:, :, :, self.at.c]
        self.waits = [self.net.send(half, half, self.at.sibling())]


class Direct:
    def __init__(self, net, at, full):
        self.net, self.at, self.full = net, at, full

    def start(self):
        at = self.at
        own = self.full.at[at.y, at.x, at.z, at.c]
        self.waits = [
            self.net.send(own, own, at.dev(*at.other(*way), at.c)) for way in at.others()
        ]

    def arrive(self):
        for copy in self.waits:
            copy.wait_recv()

    def cores(self):
        self.arrive()
        half = self.full.at[:, :, :, self.at.c]
        self.waits = [self.net.send(half, half, self.at.sibling())]


class Owners:
    def __init__(self, net, at, source, target):
        self.net, self.at, self.source, self.target = net, at, source, target
        self.first = net.slots(4)

    def copy(self, k, sender):
        first = self.first
        return self.net.copy(
            self.source(k), self.target(k), self.at.toward(k), first + k, first + sender
        )

    def send(self, k):
        @pl.when(self.at.z != k)
        def _():
            self.copy(k, self.at.z).start()

    def arrive(self):
        for step in (1, 2, 3):
            sender = self.at.ahead(step)
            self.copy(sender, sender).wait_recv()

    def drain(self):
        for step in (1, 2, 3):
            self.copy(self.at.ahead(step), self.at.z).wait_send()


class Relayed:
    def __init__(self, net, at, full):
        self.net, self.at, self.full = net, at, full
        far = at.ahead(2)
        near = at.near()
        self.zs = (at.z, near, far, lax.rem(near + 2, 4))
        self.firsts, self.seconds, self.core_moves = [None] * 4, [None] * 4, [None] * 4

    def block(self, z):
        at = self.at
        return self.full.at[at.y, at.x, z, at.c]

    def first(self, k):
        at = self.at
        block = self.block(self.zs[k])
        self.firsts[k] = self.net.send(block, block, at.across_y() if k % 2 else at.across_x())

    def start(self):
        at = self.at
        own = self.block(at.z)
        self.far = self.net.send(own, own, at.toward(self.zs[2]))
        self.near = self.net.send(own, own, at.toward(self.zs[1]))
        self.first(0)

    def take_near(self):
        self.near.wait_recv()
        self.first(1)

    def take_far(self):
        self.far.wait_recv()
        block = self.block(self.zs[2])
        self.relay = self.net.send(block, block, self.at.toward(self.zs[1]))
        self.first(2)

    def take_relay(self):
        self.relay.wait_recv()
        self.first(3)

    def second(self, k):
        self.firsts[k].wait_recv()
        at, z = self.at, self.zs[k]
        if k % 2:
            blocks, peer = self.full.at[:, at.x, z, at.c], at.across_x()
        else:
            blocks, peer = self.full.at[at.y, :, z, at.c], at.across_y()
        self.seconds[k] = self.net.send(blocks, blocks, peer)

    def cores(self, k):
        self.seconds[k].wait_recv()
        blocks = self.full.at[:, :, self.zs[k], self.at.c]
        self.core_moves[k] = self.net.send(blocks, blocks, self.at.sibling())

    def done(self):
        for copy in self.core_moves:
            copy.wait_recv()


class Scatter:
    def __init__(self, net, at, part, bufs):
        self.net, self.at, self.part = net, at, part
        self.sums, self.low1, self.high1, self.low2, self.high2, self.last = bufs

    def arrive(self):
        for copy in self.waits:
            copy.wait_recv()

    def cores(self):
        at = self.at
        self.waits = [self.net.send(self.part.at[:, :, :, 1 - at.c], self.sums, at.sibling())]

    def first(self):
        self.arrive()
        at, sums, part = self.at, self.sums, self.part

        def add(i, carry):
            y, x, z = lax.div(i, 8), lax.rem(lax.div(i, 4), 2), lax.rem(i, 4)
            sums[y, x, z] = sums[y, x, z] + part[y, x, z, at.c]
            return carry

        lax.fori_loop(0, 16, add, 0)
        self.waits = [
            self.net.send(sums.at[:, 1 - at.x, 0:2], self.low1, at.across_x()),
            self.net.send(sums.at[1 - at.y, :, 2:4], self.high1, at.across_y()),
        ]

    def second(self):
        self.arrive()
        at, sums = self.at, self.sums

        def add(i, carry):
            a, b = lax.div(i, 2), lax.rem(i, 2)
            sums[a, at.x, b] = sums[a, at.x, b] + self.low1[a, b]
            sums[at.y, a, b + 2] = sums[at.y, a, b + 2] + self.high1[a, b]
            return carry

        lax.fori_loop(0, 4, add, 0)
        self.waits = [
            self.net.send(sums.at[1 - at.y, at.x, 0:2], self.low2, at.across_y()),
            self.net.send(sums.at[at.y, 1 - at.x, 2:4], self.high2, at.across_x()),
        ]

    def gathered(self):
        self.arrive()
        at, sums = self.at, self.sums
        for b in range(2):
            sums[at.y, at.x, b] = sums[at.y, at.x, b] + self.low2[b]
            sums[at.y, at.x, b + 2] = sums[at.y, at.x, b + 2] + self.high2[b]

    def along_z(self):
        self.gathered()
        at, sums = self.at, self.sums
        self.waits = [
            self.net.send(sums.at[at.y, at.x, at.ahead(s)], self.last.at[s - 1], at.along_z(s))
            for s in (1, 2, 3)
        ]

    def pair(self):
        self.gathered()
        at, sums, last = self.at, self.sums, self.last
        near = at.near()
        peer = at.toward(near)
        beyond = sums.at[at.y, at.x, lax.rem(near + 2, 4)]
        self.waits = [self.net.send(beyond, last.at[1], peer)]
        self.near = self.net.send(sums.at[at.y, at.x, near], last.at[0], peer)

    def far(self):
        self.arrive()
        at, sums, last = self.at, self.sums, self.last
        far = at.ahead(2)
        sums[at.y, at.x, far] = sums[at.y, at.x, far] + last[1]
        self.waits = [
            self.near,
            self.net.send(sums.at[at.y, at.x, far], last.at[2], at.toward(far)),
        ]

    def total(self):
        self.arrive()
        at = self.at
        total = self.sums[at.y, at.x, at.z].astype(F32)
        return total + self.last[0].astype(F32) + self.last[2].astype(F32)


class DirectScatter:
    def __init__(self, net, at, part, sums, landed):
        self.net, self.at, self.part, self.sums, self.landed = net, at, part, sums, landed

    def cores(self):
        at = self.at
        self.move = self.net.send(self.part.at[:, :, :, 1 - at.c], self.sums, at.sibling())

    def start(self):
        self.move.wait_recv()
        at, sums = self.at, self.sums
        sums[...] = sums[...] + self.part[:, :, :, at.c]
        self.waits = []
        for i, way in enumerate(at.others()):
            y, x, z = at.other(*way)
            self.waits.append(
                self.net.send(sums.at[y, x, z], self.landed.at[i], at.dev(y, x, z, at.c))
            )

    def total(self):
        at = self.at
        total = self.sums[at.y, at.x, at.z].astype(F32)
        for i, copy in enumerate(self.waits):
            copy.wait_recv()
            total = total + self.landed[i].astype(F32)
        return total


def spread(ref, value, width):
    for j in range(width):
        ref[pl.ds(j, value.shape[0], stride=width), :] = value[:, 128 * j : 128 * j + 128]


def norm_parts(hidden):
    centered = hidden - jnp.mean(hidden, axis=-1, keepdims=True)
    spread_of = jnp.mean(centered * centered, axis=-1, keepdims=True)
    inverse = lax.rsqrt(spread_of + EPSILON)
    return centered * inverse, inverse


def norm_back(upstream, gain_row, normal, inverse):
    scaled = upstream * gain_row
    return inverse * (
        scaled
        - jnp.mean(scaled, axis=-1, keepdims=True)
        - normal * jnp.mean(scaled * normal, axis=-1, keepdims=True)
    )


def column_sum(value):
    return jnp.sum(value, axis=0, keepdims=True)


SHARDS = dict(emb=(48, 128), qkv=(16, 384), out=(16, 512), up=(16, 2048), down=(64, 512))


INPUTS = [
    "stream",
    "ids",
    "cot",
    "emb",
    "qkv",
    "out",
    "up",
    "down",
    "gains",
    "shifts",
    "outs",
    "ubias",
    "rel",
]
OUTPUTS = ["act", "gstream", "o_emb", "o_qkv", "o_out", "o_up", "o_down", "o_small"]


def scratch():
    vm = pltpu.VMEM
    s = dict(
        lin32=vm((256, 128), F32),
        emb32=vm((1024, 128), F32),
        qkv_src=vm((4, 16, 384), BF16),
        small32=vm((512, 128), F32),
        select=vm((3, 128, 512), BF16),
        landed=vm((15, 48, 128), BF16),
        vecs=vm((16, 512), F32),
        rel_row=vm((1, 256), F32),
        bias_row=vm((1, 2048), F32),
        picks=vm((256, 128), BF16),
        start=vm((128, 512), F32),
        normal1=vm((128, 512), F32),
        inverse1=vm((128, 1), F32),
        normed1=vm((4, 128, 512), BF16),
        query=vm((4, 128, 128), BF16),
        keyval=vm((2, 4, 2, 128, 128), BF16),
        probs=vm((2, 128, 2560), F32),
        mixed_out=vm((4, 128, 128), BF16),
        mixed=vm((128, 512), BF16),
        middle=vm((128, 512), F32),
        normal2=vm((128, 512), F32),
        inverse2=vm((128, 1), F32),
        normed2=vm((128, 512), BF16),
        acc1=vm((128, 512), F32),
        acc2=vm((128, 512), F32),
        gub=vm((1, 2048), F32),
        grad_mid=vm((128, 512), F32),
        gmix_src=vm((128, 512), BF16),
        gmix=vm((4, 128, 128), BF16),
        dkv=vm((2, 4, 2, 128, 128), F32),
        dkv_in=vm((2, 4, 128, 128), F32),
        slope=vm((128, 2048), F32),
        dproj=vm((4, 128, 384), BF16),
        gnorm=vm((4, 128, 512), BF16),
        gnorm_in=vm((4, 128, 512), BF16),
        sg=vm((16, 512), F32),
        gathered=vm((4, 16, 384), BF16),
    )
    for name, shard in SHARDS.items():
        s["w_" + name] = vm((2, 2, 4, 2) + shard, BF16)
        s["g_" + name] = vm((2, 2, 4, 2) + shard, BF16)
        s["r0_" + name] = vm((2, 2, 4) + shard, BF16)
        s["r1_" + name] = vm((2, 2) + shard, BF16)
        s["r2_" + name] = vm((2, 2) + shard, BF16)
        s["r3_" + name] = vm((2,) + shard, BF16)
        s["r4_" + name] = vm((2,) + shard, BF16)
        s["r5_" + name] = vm((3,) + shard, BF16)
    for name, shape, kind in (
        ("stream", (ROWS, D), BF16),
        ("ids", (1, ROWS), jnp.int32),
        ("cot", (ROWS, D), BF16),
        ("emb", (32, 128), BF16),
        ("qkv", (192, 128), BF16),
        ("out", (64, 128), BF16),
        ("up", (256, 128), BF16),
        ("down", (256, 128), BF16),
        ("gains", (1, 32), BF16),
        ("shifts", (1, 32), BF16),
        ("outs", (1, 32), BF16),
        ("ubias", (1, 64), BF16),
        ("rel", (1, 8), BF16),
    ):
        s[name] = vm(shape, kind)
    s["in_sems"] = pltpu.SemaphoreType.DMA((len(INPUTS),))
    s["send_sems"] = pltpu.SemaphoreType.DMA((240,))
    s["recv_sems"] = pltpu.SemaphoreType.DMA((240,))
    return s


def fused_kernel(*refs):
    hbm = ["h_" + name for name in INPUTS]
    names = hbm + OUTPUTS + list(scratch())
    v = types.SimpleNamespace(**dict(zip(names, refs, strict=True)))
    at = Place()
    net = Net(v.send_sems, v.recv_sems)
    y, x, z, c = at.y, at.x, at.z, at.c

    loads = {}
    for i, name in enumerate(INPUTS):
        loads[name] = pltpu.make_async_copy(
            getattr(v, "h_" + name), getattr(v, name), v.in_sems.at[i]
        )
        loads[name].start()
    barrier = pltpu.get_barrier_semaphore()
    peers = [at.dev(*at.other(*way), c) for way in at.others()] + [at.sibling()]
    for peer in peers:
        pl.semaphore_signal(
            barrier, inc=1, device_id=peer, device_id_type=pl.DeviceIdType.MESH
        )

    for name in ("emb", "gains", "shifts", "outs", "ubias", "rel"):
        loads[name].wait()
    v.small32[...] = jnp.zeros((512, 128), F32)
    for i, piece in enumerate((v.gains, v.shifts, v.outs, v.ubias, v.rel)):
        v.small32[i : i + 1, 0 : piece.shape[1]] = piece[...].astype(F32)
    v.w_emb[y, x, z, c, 0:32] = v.emb[...]
    v.w_emb[y, x, z, c, 32:48] = v.small32[0:16, :].astype(BF16)
    pl.semaphore_wait(barrier, len(peers))
    emb = Direct(net, at, v.w_emb)
    emb.start()

    loads["qkv"].wait()
    v.lin32[0:192, :] = v.qkv[...].astype(F32)
    for t in range(3):
        for zz in range(4):
            piece = v.lin32[pl.ds(4 * t + zz, 16, stride=12), :].astype(BF16)
            v.qkv_src[zz, :, 128 * t : 128 * t + 128] = piece
    v.w_qkv[y, x, z, c] = v.qkv_src[z]
    qkv = Gather(net, at, v.w_qkv, v.qkv_src)
    qkv.along_z()
    slow = []
    for name, rows, width in (("out", 16, 4), ("up", 16, 16), ("down", 64, 4)):
        loads[name].wait()
        full = getattr(v, "w_" + name)
        v.lin32[0 : rows * width, :] = getattr(v, name)[...].astype(F32)
        for j in range(width):
            full[y, x, z, c, :, 128 * j : 128 * j + 128] = v.lin32[
                pl.ds(j, rows, stride=width), :
            ].astype(BF16)
        slow.append(Relayed(net, at, full))
        slow[-1].start()
    out, up, down = slow

    lane = lax.broadcasted_iota(jnp.int32, (128, 512), 1)
    row = lax.broadcasted_iota(jnp.int32, (128, 512), 0)
    for i, size in enumerate((32, 64, 8)):
        v.select[i] = (lax.rem(lane, size) == row).astype(F32).astype(BF16)
    loads["ids"].wait()
    v.picks[...] = (
        (lax.broadcasted_iota(jnp.int32, (VOCAB, ROWS), 0) == v.ids[...]).astype(F32).astype(BF16)
    )
    emb.cores()
    qkv.first()
    loads["stream"].wait()
    loads["cot"].wait()
    emb.arrive()

    v.emb32[...] = v.w_emb[:, :, :, :, 0:32, :].reshape(1024, 128).astype(F32)
    v.small32[...] = v.w_emb[:, :, :, :, 32:48, :].reshape(512, 128).astype(F32)
    owner = lax.broadcasted_iota(jnp.int32, (32, 512), 0)
    where = lax.broadcasted_iota(jnp.int32, (32, 512), 1)

    def tiled(kind, select):
        pieces = v.small32[pl.ds(kind, 32, stride=16), :].astype(BF16)
        return dot_nn(pieces, v.select[select])

    def picked(wide, size, first):
        return column_sum(jnp.where(owner == first + lax.div(where, size), wide, 0.0))

    def halves(kind):
        wide = tiled(kind, 0)
        for half in range(2):
            v.vecs[2 * kind + half : 2 * kind + half + 1, :] = picked(wide, 32, 16 * half)

    halves(0)
    halves(1)
    for j in range(4):
        cut = slice(128 * j, 128 * j + 128)
        table = v.emb32[pl.ds(j, VOCAB, stride=4), :].astype(BF16)
        v.start[:, cut] = v.stream[:, cut].astype(F32) + dot_tn(v.picks[...], table)
    normal, inverse = norm_parts(v.start[...])
    v.normal1[...] = normal
    v.inverse1[...] = inverse
    v.normed1[z] = (normal * v.vecs[0:1, :] + v.vecs[2:3, :]).astype(BF16)
    normed_moves = [None] + [
        net.send(v.normed1.at[z], v.normed1.at[z], at.along_z(s)) for s in (1, 2, 3)
    ]
    qkv.second()
    for g in slow:
        g.take_near()
        g.take_far()
    halves(2)
    wide = tiled(3, 1)
    for block in range(4):
        v.bias_row[:, 512 * block : 512 * block + 512] = picked(wide, 64, 8 * block)
    rel_row = picked(tiled(4, 2), 8, 0)[:, 0:256]
    rel_lane = lax.broadcasted_iota(jnp.int32, (1, 256), 1)
    qkv.cores()
    for g in slow:
        g.second(0)
    for g in slow:
        g.take_relay()
    for g in slow:
        g.second(1)

    qkv.arrive()
    weight = v.w_qkv[...].reshape(512, 384)
    moves = []
    for s in range(4):
        if s:
            normed_moves[s].wait_recv()
        zs = at.behind(s)
        projected = dot_nn(v.normed1[zs], weight).astype(BF16)
        v.query[zs] = projected[:, 0:128]
        v.keyval[0, zs, c] = projected[:, 128:256]
        v.keyval[1, zs, c] = projected[:, 256:384]
        both = v.keyval.at[:, zs, c]
        moves.append(net.send(both, both, at.sibling()))
        if s == 1:
            for g in slow:
                g.second(2)
        if s == 2:
            for g in slow:
                g.second(3)
                g.cores(0)
    for copy in moves:
        copy.wait_recv()

    pair_lane = lax.broadcasted_iota(jnp.int32, (ROWS, PAIR), 1)
    head_lanes = (pair_lane < HEAD_DIM, pair_lane >= HEAD_DIM)

    def rel_value(head, distance):
        spot = (2 * z + head) * BUCKETS + distance
        return jnp.sum(jnp.where(rel_lane == spot, rel_row, 0.0), axis=1, keepdims=True)

    rel_values = [[rel_value(h, d) for d in range(4)] for h in range(2)]
    zero = jnp.zeros((), BF16)
    own_lanes = pl.ds(pl.multiple_of(z * PAIR, PAIR), PAIR)
    to_owner = Owners(net, at, lambda k: v.mixed_out.at[k], lambda k: v.mixed.at[:, own_lanes])
    for zq in range(4):
        count = 256 * (zq + 1)
        keys = v.keyval[0, 0 : zq + 1].reshape(count, PAIR)
        vals = v.keyval[1, 0 : zq + 1].reshape(count, PAIR)
        heads = []
        for h in range(2):
            query = jnp.where(head_lanes[h], v.query[zq], zero)
            bias = jnp.concatenate(
                [
                    jnp.broadcast_to(rel_values[h][zq - zk], (1, 256))
                    for zk in range(zq + 1)
                ],
                axis=1,
            )
            scores = dot_nt(query, keys) * SCALING + bias
            shifted = jnp.exp(scores - jnp.max(scores, axis=-1, keepdims=True))
            probs = shifted / jnp.sum(shifted, axis=-1, keepdims=True)
            v.probs[h, :, KEYS_AT[zq] : KEYS_AT[zq] + count] = probs
            heads.append(dot_nn(probs.astype(BF16), vals))
        v.mixed_out[zq] = jnp.where(head_lanes[0], heads[0], heads[1]).astype(BF16)
        to_owner.send(zq)
    v.mixed[:, own_lanes] = v.mixed_out[z]
    for k in (1, 2, 3):
        for g in slow:
            g.cores(k)
    to_owner.arrive()

    out.done()
    mixed = v.mixed[...]
    out_weight = v.w_out[...].reshape(512, 512)
    middle = v.start[...] + dot_nn(mixed, out_weight) + v.vecs[4:5, :]
    v.middle[...] = middle
    normal, inverse = norm_parts(middle)
    v.normal2[...] = normal
    v.inverse2[...] = inverse
    v.normed2[...] = (normal * v.vecs[1:2, :] + v.vecs[3:4, :]).astype(BF16)
    v.acc1[...] = jnp.zeros_like(v.acc1)
    v.acc2[...] = jnp.zeros_like(v.acc2)
    up.done()
    down.done()

    def scatter(name):
        bufs = [getattr(v, f"r{i}_{name}") for i in range(6)]
        return Scatter(net, at, getattr(v, "g_" + name), bufs)

    s_down, s_up, s_out, s_qkv = (scatter(n) for n in ("down", "up", "out", "qkv"))
    s_emb = DirectScatter(net, at, v.g_emb, v.r0_emb, v.landed)

    def forward_tile(i, carry):
        cols = pl.ds(pl.multiple_of(i * 256, 256), 256)
        ty, tx, tz = lax.div(i, 4), lax.rem(lax.div(i, 2), 2), lax.rem(i, 2) * 2
        up_tile = v.w_up[:, :, :, :, :, cols].reshape(512, 256)
        down_tile = v.w_down[ty, tx, pl.ds(tz, 2)].reshape(256, 512)
        lifted = dot_nn(v.normed2[...], up_tile) + v.bias_row[:, cols]
        share = 0.5 * (1.0 + lax.erf(lifted * ROOT_HALF))
        active = (lifted * share).astype(BF16)
        v.slope[:, cols] = share + lifted * (jnp.exp(-0.5 * lifted * lifted) * ROOT_TAU)
        v.acc1[...] += dot_nn(active, down_tile)
        v.g_down[ty, tx, pl.ds(tz, 2)] = (
            dot_tn(active, v.cot[...]).astype(BF16).reshape(2, 2, 64, 512)
        )
        return carry

    lax.fori_loop(0, 8, forward_tile, 0)
    s_down.cores()

    def backward_tile(i, carry):
        cols = pl.ds(pl.multiple_of(i * 256, 256), 256)
        ty, tx, tz = lax.div(i, 4), lax.rem(lax.div(i, 2), 2), lax.rem(i, 2) * 2
        up_tile = v.w_up[:, :, :, :, :, cols].reshape(512, 256)
        down_tile = v.w_down[ty, tx, pl.ds(tz, 2)].reshape(256, 512)
        grad_lifted = dot_nt(v.cot[...], down_tile) * v.slope[:, cols]
        v.gub[:, cols] = column_sum(grad_lifted)
        low = grad_lifted.astype(BF16)
        v.acc2[...] += dot_nt(low, up_tile)
        v.g_up[:, :, :, :, :, cols] = (
            dot_tn(v.normed2[...], low).astype(BF16).reshape(2, 2, 4, 2, 16, 256)
        )
        return carry

    lax.fori_loop(0, 8, backward_tile, 0)
    s_up.cores()
    grad_wide = v.cot[...].astype(F32)
    upstream = v.acc2[...]
    normal = v.normal2[...]
    grad_middle = grad_wide + norm_back(upstream, v.vecs[1:2, :], normal, v.inverse2[...])
    v.grad_mid[...] = grad_middle
    middle_low = grad_middle.astype(BF16)
    v.gmix_src[...] = dot_nt(middle_low, v.w_out[...].reshape(512, 512)).astype(BF16)
    moves = [
        net.send(
            v.gmix_src.at[:, pl.ds(pl.multiple_of(at.ahead(s) * PAIR, PAIR), PAIR)],
            v.gmix.at[z],
            at.along_z(s),
        )
        for s in (1, 2, 3)
    ]
    v.gmix[z] = v.gmix_src[:, own_lanes]
    v.g_out[...] = dot_tn(v.mixed[...], middle_low).astype(BF16).reshape(2, 2, 4, 2, 16, 512)
    s_out.cores()
    s_down.first()
    v.sg[1:2, :] = column_sum(upstream * normal)
    v.sg[3:4, :] = column_sum(upstream)
    v.sg[4:5, :] = column_sum(grad_middle)
    v.sg[5:6, :] = column_sum(grad_wide)
    v.act[...] = (v.middle[...] + v.acc1[...] + v.vecs[5:6, :]).astype(BF16)
    s_up.first()
    s_out.first()
    for copy in moves:
        copy.wait_recv()

    rel_sums = [[jnp.zeros((1, 256), F32) for d in range(4)] for h in range(2)]
    weight = v.w_qkv[...].reshape(512, 384)
    core_moves = {}
    gnorm_out = Owners(net, at, lambda k: v.gnorm.at[k], lambda k: v.gnorm_in.at[z])

    def project_back(zq):
        core_moves[zq].wait_recv()
        dkeys = (v.dkv[0, zq, c] + v.dkv_in[0, zq]) * SCALING
        dvals = v.dkv[1, zq, c] + v.dkv_in[1, zq]
        v.dproj[zq, :, 128:256] = dkeys.astype(BF16)
        v.dproj[zq, :, 256:384] = dvals.astype(BF16)
        v.gnorm[zq] = dot_nt(v.dproj[zq], weight).astype(BF16)
        gnorm_out.send(zq)

    for zq in (3, 2, 1, 0):
        count = 256 * (zq + 1)
        keys = v.keyval[0, 0 : zq + 1].reshape(count, PAIR)
        vals = v.keyval[1, 0 : zq + 1].reshape(count, PAIR)
        heads, dkeys, dvals = [], 0.0, 0.0
        for h in range(2):
            query = jnp.where(head_lanes[h], v.query[zq], zero)
            grad = jnp.where(head_lanes[h], v.gmix[zq], zero)
            probs = v.probs[h, :, KEYS_AT[zq] : KEYS_AT[zq] + count]
            grad_probs = dot_nt(grad, vals)
            inner = jnp.sum(probs * grad_probs, axis=-1, keepdims=True)
            grad_scores = probs * (grad_probs - inner)
            for zk in range(zq + 1):
                tile = grad_scores[:, 256 * zk : 256 * zk + 256]
                rel_sums[h][zq - zk] = rel_sums[h][zq - zk] + column_sum(tile)
            low = grad_scores.astype(BF16)
            heads.append(dot_nn(low, keys))
            dkeys = dkeys + dot_tn(low, query)
            dvals = dvals + dot_tn(probs.astype(BF16), grad)
        v.dproj[zq, :, 0:128] = (
            jnp.where(head_lanes[0], heads[0], heads[1]) * SCALING
        ).astype(BF16)
        dkeys = dkeys.reshape(zq + 1, 2, ROWS, PAIR)
        dvals = dvals.reshape(zq + 1, 2, ROWS, PAIR)
        if zq == 3:
            v.dkv[0] = dkeys
            v.dkv[1] = dvals
        else:
            v.dkv[0, 0 : zq + 1] += dkeys
            v.dkv[1, 0 : zq + 1] += dvals
        core_moves[zq] = net.send(
            v.dkv.at[:, zq, 1 - c], v.dkv_in.at[:, zq], at.sibling()
        )
        if zq < 3:
            project_back(zq + 1)
        if zq == 1:
            s_down.second()
    project_back(0)
    s_up.second()
    s_out.second()
    v.g_qkv[...] = (
        dot_tn(v.normed1[...].reshape(512, 512), v.dproj[...].reshape(512, 384))
        .astype(BF16)
        .reshape(2, 2, 4, 2, 16, 384)
    )
    s_qkv.cores()
    s_down.pair()

    sums = jnp.zeros((1, 512), F32)
    wide_lane = lax.broadcasted_iota(jnp.int32, (1, 512), 1)
    for h in range(2):
        for d in range(4):
            spot = (2 * z + h) * BUCKETS + d
            value = jnp.sum(rel_sums[h][d], axis=1, keepdims=True)
            sums = sums + jnp.where(wide_lane == spot, value, 0.0)

    def cut(kind, select, size, lines):
        wide = jnp.zeros((32, 512), F32)
        for i, line in enumerate(lines):
            first = (512 // size) * i
            wide = jnp.where(owner == first + lax.div(where, size), line, wide)
        v.small32[pl.ds(kind, 32, stride=16), :] = dot_nt(wide.astype(BF16), v.select[select])

    v.small32[...] = jnp.zeros((512, 128), F32)
    cut(2, 0, 32, [v.sg[4:5, :], v.sg[5:6, :]])
    cut(3, 1, 64, [v.gub[:, 512 * i : 512 * i + 512] for i in range(4)])
    cut(4, 2, 8, [sums])
    s_qkv.first()

    gnorm_out.arrive()
    upstream = v.gnorm[z].astype(F32)
    for s in (1, 2, 3):
        upstream = upstream + v.gnorm_in[at.ahead(s)].astype(F32)
    normal = v.normal1[...]
    grad_start = v.grad_mid[...] + norm_back(upstream, v.vecs[0:1, :], normal, v.inverse1[...])
    start_low = grad_start.astype(BF16)
    spread(v.emb32, dot_nn(v.picks[...], start_low), 4)
    v.g_emb[:, :, :, :, 0:32, :] = v.emb32[...].astype(BF16).reshape(2, 2, 4, 2, 32, 128)
    cut(0, 0, 32, [column_sum(upstream * normal), v.sg[1:2, :]])
    cut(1, 0, 32, [column_sum(upstream), v.sg[3:4, :]])
    v.g_emb[:, :, :, :, 32:48, :] = v.small32[...].astype(BF16).reshape(2, 2, 4, 2, 16, 128)
    s_emb.cores()
    v.gstream[...] = start_low
    s_up.pair()
    s_out.pair()
    s_emb.start()
    s_down.far()
    s_qkv.second()
    s_up.far()
    s_out.far()
    s_qkv.along_z()
    spread(v.o_down, s_down.total(), 4)
    total = s_emb.total()
    v.o_emb[...] = total[0:32]
    v.o_small[...] = total[32:40]
    spread(v.o_up, s_up.total(), 16)
    spread(v.o_out, s_out.total(), 4)
    s_qkv.arrive()
    v.gathered[z] = v.r0_qkv[y, x, z]
    for s in (1, 2, 3):
        v.gathered[at.behind(s)] = v.r5_qkv[s - 1]
    for zz in range(4):
        piece = v.gathered[zz].astype(F32)
        for t in range(3):
            v.o_qkv[pl.ds(4 * t + zz, 16, stride=12), :] = piece[:, 128 * t : 128 * t + 128]
    to_owner.drain()
    gnorm_out.drain()
    net.drain()


def store_kernel(*refs):
    ins, small, outs, sems = refs[:7], refs[7], refs[8:20], refs[20]
    copies = [pltpu.make_async_copy(ins[i], outs[i], sems.at[i]) for i in range(7)]
    for copy in copies:
        copy.start()
    for i in range(5):
        outs[7 + i][...] = small[i : i + 1, 0 : outs[7 + i].shape[1]]
    for copy in copies:
        copy.wait()


def fused_local(
    stream,
    byte_ids,
    cotangent,
    embed_flat,
    qkv_flat,
    out_flat,
    up_flat,
    down_flat,
    gains,
    norm_shifts,
    out_shifts,
    up_bias,
    rel_bias,
):
    operands = (
        stream.reshape(ROWS, D),
        byte_ids,
        cotangent.reshape(ROWS, D),
        embed_flat.reshape(-1, 128),
        qkv_flat.reshape(-1, 128),
        out_flat.reshape(-1, 128),
        up_flat.reshape(-1, 128),
        down_flat.reshape(-1, 128),
        gains.reshape(1, -1),
        norm_shifts.reshape(1, -1),
        out_shifts.reshape(1, -1),
        up_bias.reshape(1, -1),
        rel_bias.reshape(1, -1),
    )
    shapes = (
        ((ROWS, D), BF16),
        ((ROWS, D), BF16),
        ((32, 128), F32),
        ((192, 128), F32),
        ((64, 128), F32),
        ((256, 128), F32),
        ((256, 128), F32),
        ((8, 128), F32),
    )
    whole = pl.BlockSpec(memory_space=pltpu.VMEM)
    anywhere = pl.BlockSpec(memory_space=pl.ANY)
    results = pl.pallas_call(
        fused_kernel,
        out_shape=[jax.ShapeDtypeStruct(s, t) for s, t in shapes],
        in_specs=[pl.BlockSpec(memory_space=pltpu.HBM)] * len(operands),
        out_specs=[whole] * len(shapes),
        scratch_shapes=list(scratch().values()),
        compiler_params=pltpu.CompilerParams(
            collective_id=0, has_side_effects=True, vmem_limit_bytes=32 << 20
        ),
        name="layer",
    )(*operands)
    vectors = (gains, norm_shifts, out_shifts, up_bias, rel_bias)
    small_shapes = [((1, p.shape[0]), F32) for p in vectors]
    final = pl.pallas_call(
        store_kernel,
        out_shape=[jax.ShapeDtypeStruct(s, t) for s, t in shapes[:7] + tuple(small_shapes)],
        in_specs=[whole] * 8,
        out_specs=[anywhere] * 7 + [whole] * 5,
        scratch_shapes=[pltpu.SemaphoreType.DMA((7,))],
        compiler_params=pltpu.CompilerParams(vmem_limit_bytes=8 << 20),
        name="store",
    )(*results)
    return (
        final[0].reshape(stream.shape),
        final[1].reshape(stream.shape),
        *(part.reshape(-1) for part in final[2:]),
    )


def solution(mesh):
    body = fused_local if (mesh.shape["dp"], mesh.shape["seq"]) == (4, 8) else local
    in_specs = (
        P("dp", "seq", None),
        P("dp", "seq"),
        P("dp", "seq", None),
        P(("dp", "seq")),
        P(("dp", "seq")),
        P(("dp", "seq")),
        P(("dp", "seq")),
        P(("dp", "seq")),
        P(("dp", "seq")),
        P(("dp", "seq")),
        P(("dp", "seq")),
        P(("dp", "seq")),
        P(("dp", "seq")),
    )
    out_specs = (
        P("dp", "seq", None),
        P("dp", "seq", None),
        P(("dp", "seq")),
        P(("dp", "seq")),
        P(("dp", "seq")),
        P(("dp", "seq")),
        P(("dp", "seq")),
        P(("dp", "seq")),
        P(("dp", "seq")),
        P(("dp", "seq")),
        P(("dp", "seq")),
        P(("dp", "seq")),
    )
    return jax.shard_map(body, mesh=mesh, in_specs=in_specs, out_specs=out_specs, check_vma=False)
```

```python
import types

import jax
import jax.numpy as jnp
from jax import lax
from jax.experimental import pallas as pl
from jax.experimental.pallas import tpu as pltpu
from jax.sharding import PartitionSpec as P

D = 512
HEADS = 8
HEAD_DIM = 64
FF = 2048
VOCAB = 256
BLOCK = 256
BUCKETS = 32


EPSILON = 1e-05
SCALING = 0.125
MASKED = -1e30


def layer_norm(hidden, gain_row, shift_row):
    centered = hidden - jnp.mean(hidden, axis=-1, keepdims=True)
    spread = jnp.mean(centered * centered, axis=-1, keepdims=True)
    return centered * lax.rsqrt(spread + EPSILON) * gain_row + shift_row


def gelu_exact(values):
    return jax.nn.gelu(values, approximate=False)


def unpack(gathered):
    embed, w_qkv, w_out, w_up, w_down, gain_flat, norm_flat, out_flat, bias_flat, rel_flat = (
        gathered
    )
    return (
        embed.reshape(VOCAB, D),
        w_qkv.reshape(D, 3 * D),
        w_out.reshape(D, D),
        w_up.reshape(D, FF),
        w_down.reshape(FF, D),
        gain_flat.astype(jnp.float32).reshape(2, D),
        norm_flat.astype(jnp.float32).reshape(2, D),
        out_flat.astype(jnp.float32).reshape(2, D),
        bias_flat.astype(jnp.float32),
        rel_flat.astype(jnp.float32).reshape(HEADS, BUCKETS),
    )


def block_terms(rel_table, row_first, row_count, key_first, key_count):
    row_blocks = max(row_count // BLOCK, 1)
    key_blocks = max(key_count // BLOCK, 1)
    row_ids = row_first // BLOCK + jnp.arange(row_blocks, dtype=jnp.int32)
    key_ids = key_first // BLOCK + jnp.arange(key_blocks, dtype=jnp.int32)
    distance = row_ids[:, None] - key_ids[None, :]
    allowed = distance >= 0
    bucket = jnp.clip(distance, 0, BUCKETS - 1)
    selector = (bucket[:, :, None] == jnp.arange(BUCKETS, dtype=jnp.int32)[None, None, :]).astype(
        jnp.float32
    )
    bias_tiles = jnp.einsum("abn,hn->hab", selector, rel_table, precision=lax.Precision.HIGHEST)
    return (bias_tiles, allowed, selector)


def score_tile(query_heads, key_heads, bias_tiles, allowed):
    row_count = query_heads.shape[0]
    key_count = key_heads.shape[0]
    raw_scores = (
        jnp.einsum("qhd,khd->hqk", query_heads, key_heads, preferred_element_type=jnp.float32)
        * SCALING
    )
    row_blocks = bias_tiles.shape[1]
    key_blocks = bias_tiles.shape[2]
    tiled = raw_scores.reshape(
        HEADS, row_blocks, row_count // row_blocks, key_blocks, key_count // key_blocks
    )
    tiled = tiled + bias_tiles[:, :, None, :, None]
    tiled = jnp.where(allowed[None, :, None, :, None], tiled, MASKED)
    return tiled.reshape(HEADS, row_count, key_count)


def heads_of(rows):
    return rows.reshape(rows.shape[0], HEADS, HEAD_DIM)


def attend(queries, key_rows, value_rows, bias_tiles, allowed):
    local_rows = queries.shape[0]
    scores = score_tile(heads_of(queries), heads_of(key_rows), bias_tiles, allowed)
    row_max = jnp.max(scores, axis=-1, keepdims=True)
    shifted = jnp.exp(scores - row_max)
    row_sum = jnp.sum(shifted, axis=-1, keepdims=True)
    soft_weights = (shifted / row_sum).astype(jnp.bfloat16)
    mixed_heads = jnp.einsum(
        "hqk,khd->qhd", soft_weights, heads_of(value_rows), preferred_element_type=jnp.float32
    )
    return (mixed_heads.reshape(local_rows, D), (row_max + jnp.log(row_sum))[:, :, 0])


def row_back(queries, key_rows, value_rows, log_totals, grad_mixed, bias_tiles, allowed, selector):
    local_rows = queries.shape[0]
    seq_length = key_rows.shape[0]
    query_heads = heads_of(queries)
    key_heads = heads_of(key_rows)
    value_heads = heads_of(value_rows)
    grad_heads = heads_of(grad_mixed)
    scores = score_tile(query_heads, key_heads, bias_tiles, allowed)
    soft_weights = jnp.exp(scores - log_totals[:, :, None])
    grad_weights = jnp.einsum(
        "qhd,khd->hqk", grad_heads, value_heads, preferred_element_type=jnp.float32
    )
    row_inner = jnp.sum(soft_weights * grad_weights, axis=-1)
    grad_scores = soft_weights * (grad_weights - row_inner[:, :, None])
    row_blocks = bias_tiles.shape[1]
    key_blocks = bias_tiles.shape[2]
    tile_sums = jnp.sum(
        grad_scores.reshape(
            HEADS, row_blocks, local_rows // row_blocks, key_blocks, seq_length // key_blocks
        ),
        axis=(2, 4),
    )
    grad_table = jnp.einsum("hab,abn->hn", tile_sums, selector, precision=lax.Precision.HIGHEST)
    scores_low = grad_scores.astype(jnp.bfloat16)
    grad_queries = (
        jnp.einsum("hqk,khd->qhd", scores_low, key_heads, preferred_element_type=jnp.float32)
        * SCALING
    )
    grad_queries = grad_queries.reshape(local_rows, D)
    grad_keys = (
        jnp.einsum("hqk,qhd->khd", scores_low, query_heads, preferred_element_type=jnp.float32)
        * SCALING
    )
    grad_values = jnp.einsum(
        "hqk,qhd->khd",
        soft_weights.astype(jnp.bfloat16),
        grad_heads,
        preferred_element_type=jnp.float32,
    )
    return (
        grad_queries,
        grad_table,
        row_inner,
        grad_keys.reshape(seq_length, D),
        grad_values.reshape(seq_length, D),
    )


def local(
    stream,
    byte_ids,
    cotangent,
    embed_flat,
    qkv_flat,
    out_flat,
    up_flat,
    down_flat,
    gains,
    norm_shifts,
    out_shifts,
    up_bias,
    rel_bias,
):
    seq_count = stream.shape[0]
    local_rows = stream.shape[1]
    seq_length = local_rows * lax.axis_size("seq")
    tokens = seq_count * local_rows
    first_row = lax.axis_index("seq") * local_rows
    owned = (
        embed_flat,
        qkv_flat,
        out_flat,
        up_flat,
        down_flat,
        gains,
        norm_shifts,
        out_shifts,
        up_bias,
        rel_bias,
    )
    gathered = (
        lax.all_gather(owned[0], ("dp", "seq"), axis=0, tiled=True),
        lax.all_gather(owned[1], ("dp", "seq"), axis=0, tiled=True),
        lax.all_gather(owned[2], ("dp", "seq"), axis=0, tiled=True),
        lax.all_gather(owned[3], ("dp", "seq"), axis=0, tiled=True),
        lax.all_gather(owned[4], ("dp", "seq"), axis=0, tiled=True),
        lax.all_gather(owned[5], ("dp", "seq"), axis=0, tiled=True),
        lax.all_gather(owned[6], ("dp", "seq"), axis=0, tiled=True),
        lax.all_gather(owned[7], ("dp", "seq"), axis=0, tiled=True),
        lax.all_gather(owned[8], ("dp", "seq"), axis=0, tiled=True),
        lax.all_gather(owned[9], ("dp", "seq"), axis=0, tiled=True),
    )
    embed, w_qkv, w_out, w_up, w_down, gain_pair, norm_pair, out_pair, bias_up, rel_table = unpack(
        gathered
    )
    picker = byte_ids.reshape(tokens, 1) == jnp.arange(VOCAB, dtype=jnp.int32)[None, :]
    embedded = jnp.dot(picker.astype(jnp.bfloat16), embed, preferred_element_type=jnp.float32)
    start_rows = stream.reshape(tokens, D).astype(jnp.float32) + embedded
    normed_wide, norm_back_one = jax.vjp(layer_norm, start_rows, gain_pair[0], norm_pair[0])
    normed_one = normed_wide.astype(jnp.bfloat16)
    projected = jnp.dot(normed_one, w_qkv, preferred_element_type=jnp.float32).astype(jnp.bfloat16)
    queries = projected[:, :D].reshape(seq_count, local_rows, D)
    key_rows = projected[:, D : 2 * D].reshape(seq_count, local_rows, D)
    value_rows = projected[:, 2 * D :].reshape(seq_count, local_rows, D)
    keys_all, values_all = (
        lax.all_gather(key_rows, "seq", axis=1, tiled=True),
        lax.all_gather(value_rows, "seq", axis=1, tiled=True),
    )
    bias_tiles, allowed, selector = block_terms(rel_table, first_row, local_rows, 0, seq_length)

    def attend_single(operands):
        return attend(operands[0], operands[1], operands[2], bias_tiles, allowed)

    mixed, log_totals = lax.map(attend_single, (queries, keys_all, values_all))
    mixed_low = mixed.reshape(tokens, D).astype(jnp.bfloat16)
    middle = (
        start_rows + jnp.dot(mixed_low, w_out, preferred_element_type=jnp.float32) + out_pair[0]
    )
    normed_mid, norm_back_two = jax.vjp(layer_norm, middle, gain_pair[1], norm_pair[1])
    normed_two = normed_mid.astype(jnp.bfloat16)
    lifted = jnp.dot(normed_two, w_up, preferred_element_type=jnp.float32) + bias_up
    activated, gelu_back = jax.vjp(gelu_exact, lifted)
    active = activated.astype(jnp.bfloat16)
    result = middle + jnp.dot(active, w_down, preferred_element_type=jnp.float32) + out_pair[1]
    gathered_again = (
        lax.all_gather(owned[0], ("dp", "seq"), axis=0, tiled=True),
        lax.all_gather(owned[1], ("dp", "seq"), axis=0, tiled=True),
        lax.all_gather(owned[2], ("dp", "seq"), axis=0, tiled=True),
        lax.all_gather(owned[3], ("dp", "seq"), axis=0, tiled=True),
        lax.all_gather(owned[4], ("dp", "seq"), axis=0, tiled=True),
        lax.all_gather(owned[5], ("dp", "seq"), axis=0, tiled=True),
        lax.all_gather(owned[6], ("dp", "seq"), axis=0, tiled=True),
        lax.all_gather(owned[7], ("dp", "seq"), axis=0, tiled=True),
        lax.all_gather(owned[8], ("dp", "seq"), axis=0, tiled=True),
        lax.all_gather(owned[9], ("dp", "seq"), axis=0, tiled=True),
    )
    embed, w_qkv, w_out, w_up, w_down, gain_pair, norm_pair, out_pair, bias_up, rel_table = unpack(
        gathered_again
    )
    grad_output = cotangent.reshape(tokens, D)
    grad_wide = grad_output.astype(jnp.float32)
    grad_shift_down = jnp.sum(grad_wide, axis=0)
    grad_w_down = jnp.einsum("tf,td->fd", active, grad_output, preferred_element_type=jnp.float32)
    grad_active = jnp.einsum("td,fd->tf", grad_output, w_down, preferred_element_type=jnp.float32)
    (grad_lifted,) = gelu_back(grad_active)
    grad_bias_up = jnp.sum(grad_lifted, axis=0)
    lifted_low = grad_lifted.astype(jnp.bfloat16)
    grad_w_up = jnp.einsum("td,tf->df", normed_two, lifted_low, preferred_element_type=jnp.float32)
    grad_normed_two = jnp.einsum("tf,df->td", lifted_low, w_up, preferred_element_type=jnp.float32)
    grad_mid_norm, grad_gain_two, grad_shift_two = norm_back_two(grad_normed_two)
    grad_middle = grad_wide + grad_mid_norm
    grad_shift_out = jnp.sum(grad_middle, axis=0)
    middle_low = grad_middle.astype(jnp.bfloat16)
    grad_w_out = jnp.einsum("te,td->ed", mixed_low, middle_low, preferred_element_type=jnp.float32)
    grad_mixed = jnp.einsum("td,ed->te", middle_low, w_out, preferred_element_type=jnp.float32)
    grad_mixed = grad_mixed.astype(jnp.bfloat16).reshape(seq_count, local_rows, D)
    keys_all, values_all = (
        lax.all_gather(key_rows, "seq", axis=1, tiled=True),
        lax.all_gather(value_rows, "seq", axis=1, tiled=True),
    )

    def back_with_keys(operands):
        return row_back(
            operands[0],
            operands[1],
            operands[2],
            operands[3],
            operands[4],
            bias_tiles,
            allowed,
            selector,
        )

    grad_queries, grad_tables, unused, grad_keys, grad_values = lax.map(
        back_with_keys, (queries, keys_all, values_all, log_totals, grad_mixed)
    )
    grad_keys, grad_values = (
        lax.psum_scatter(grad_keys, "seq", scatter_dimension=1, tiled=True),
        lax.psum_scatter(grad_values, "seq", scatter_dimension=1, tiled=True),
    )
    grad_table_all = jnp.sum(grad_tables, axis=0)
    grad_projected = jnp.concatenate([grad_queries, grad_keys, grad_values], axis=-1)
    grad_projected = grad_projected.reshape(tokens, 3 * D).astype(jnp.bfloat16)
    grad_w_qkv = jnp.einsum(
        "td,tk->dk", normed_one, grad_projected, preferred_element_type=jnp.float32
    )
    grad_normed_one = jnp.einsum(
        "tk,dk->td", grad_projected, w_qkv, preferred_element_type=jnp.float32
    )
    grad_start_norm, grad_gain_one, grad_shift_one = norm_back_one(grad_normed_one)
    grad_start = grad_middle + grad_start_norm
    grad_embed_local = jnp.einsum(
        "tv,td->vd", picker.astype(jnp.float32), grad_start, precision=lax.Precision.HIGHEST
    )
    local_grads = (
        grad_embed_local.reshape(-1),
        grad_w_qkv.reshape(-1),
        grad_w_out.reshape(-1),
        grad_w_up.reshape(-1),
        grad_w_down.reshape(-1),
        jnp.stack([grad_gain_one, grad_gain_two]).reshape(-1),
        jnp.stack([grad_shift_one, grad_shift_two]).reshape(-1),
        jnp.stack([grad_shift_out, grad_shift_down]).reshape(-1),
        grad_bias_up,
        grad_table_all.reshape(-1),
    )
    summed = (
        lax.psum_scatter(local_grads[0], ("dp", "seq"), scatter_dimension=0, tiled=True),
        lax.psum_scatter(local_grads[1], ("dp", "seq"), scatter_dimension=0, tiled=True),
        lax.psum_scatter(local_grads[2], ("dp", "seq"), scatter_dimension=0, tiled=True),
        lax.psum_scatter(local_grads[3], ("dp", "seq"), scatter_dimension=0, tiled=True),
        lax.psum_scatter(local_grads[4], ("dp", "seq"), scatter_dimension=0, tiled=True),
        lax.psum_scatter(local_grads[5], ("dp", "seq"), scatter_dimension=0, tiled=True),
        lax.psum_scatter(local_grads[6], ("dp", "seq"), scatter_dimension=0, tiled=True),
        lax.psum_scatter(local_grads[7], ("dp", "seq"), scatter_dimension=0, tiled=True),
        lax.psum_scatter(local_grads[8], ("dp", "seq"), scatter_dimension=0, tiled=True),
        lax.psum_scatter(local_grads[9], ("dp", "seq"), scatter_dimension=0, tiled=True),
    )
    return (
        result.reshape(seq_count, local_rows, D).astype(jnp.bfloat16),
        grad_start.reshape(seq_count, local_rows, D).astype(jnp.bfloat16),
        summed[0],
        summed[1],
        summed[2],
        summed[3],
        summed[4],
        summed[5],
        summed[6],
        summed[7],
        summed[8],
        summed[9],
    )


BF16 = jnp.bfloat16
F32 = jnp.float32
ROWS = 128
PAIR = 128
KEYS_AT = (0, 256, 768, 1536)
ROOT_HALF = 0.7071067811865476
ROOT_TAU = 0.3989422804014327


def dot_nn(a, b):
    return jnp.dot(a, b, preferred_element_type=F32)


def dot_nt(a, b):
    return lax.dot_general(a, b, (((1,), (1,)), ((), ())), preferred_element_type=F32)


def dot_tn(a, b):
    return lax.dot_general(a, b, (((0,), (0,)), ((), ())), preferred_element_type=F32)


class Net:
    def __init__(self, send_sems, recv_sems):
        self.send_sems, self.recv_sems, self.copies = send_sems, recv_sems, []

    def send(self, src, dst, device):
        at = len(self.copies)
        copy = pltpu.make_async_remote_copy(
            src_ref=src,
            dst_ref=dst,
            send_sem=self.send_sems.at[at],
            recv_sem=self.recv_sems.at[at],
            device_id=device,
            device_id_type=pl.DeviceIdType.MESH,
        )
        copy.start()
        self.copies.append(copy)
        return copy

    def slots(self, count):
        first = len(self.copies)
        self.copies.extend([None] * count)
        return first

    def copy(self, src, dst, device, send_at, recv_at):
        return pltpu.make_async_remote_copy(
            src_ref=src,
            dst_ref=dst,
            send_sem=self.send_sems.at[send_at],
            recv_sem=self.recv_sems.at[recv_at],
            device_id=device,
            device_id_type=pl.DeviceIdType.MESH,
        )

    def drain(self):
        for copy in self.copies:
            if copy is not None:
                copy.wait_send()


class Place:
    def __init__(self):
        dp, seq = lax.axis_index("dp"), lax.axis_index("seq")
        self.dp, self.seq = dp, seq
        self.y, self.x = lax.div(dp, 2), lax.rem(dp, 2)
        self.z, self.c = lax.div(seq, 2), lax.rem(seq, 2)
        self.flat = dp * 8 + seq

    def dev(self, y, x, z, c):
        return (y * 2 + x, z * 2 + c)

    def sibling(self):
        return self.dev(self.y, self.x, self.z, 1 - self.c)

    def across_x(self):
        return self.dev(self.y, 1 - self.x, self.z, self.c)

    def across_y(self):
        return self.dev(1 - self.y, self.x, self.z, self.c)

    def across_xy(self):
        return self.dev(1 - self.y, 1 - self.x, self.z, self.c)

    def line(self):
        near = self.near()
        return self.z, near, self.ahead(2), lax.rem(near + 2, 4)

    def near(self):
        return self.z + 1 - 2 * lax.rem(self.z, 2)

    def toward(self, z):
        return self.dev(self.y, self.x, z, self.c)

    def others(self):
        return [
            (dy, dx, dz) for dz in (2, 1, 3, 0) for dy in (1, 0) for dx in (1, 0) if dy + dx + dz
        ]

    def other(self, dy, dx, dz):
        y = 1 - self.y if dy else self.y
        x = 1 - self.x if dx else self.x
        return y, x, self.ahead(dz)

    def ahead(self, step):
        return lax.rem(self.z + step, 4)

    def behind(self, step):
        return lax.rem(self.z + (4 - step), 4)

    def along_z(self, step):
        return self.dev(self.y, self.x, self.ahead(step), self.c)


class Columns:
    def __init__(self, net, at, full, sources):
        self.net, self.at, self.full, self.sources = net, at, full, sources

    def along_z(self):
        at = self.at
        own = self.full.at[at.y, at.x, at.z, at.c]
        self.waits = [
            self.net.send(self.sources.at[at.ahead(s)], own, at.along_z(s)) for s in (2, 1, 3)
        ]

    def arrive(self):
        for copy in self.waits:
            copy.wait_recv()

    def plane(self):
        self.arrive()
        at = self.at
        blocks = self.full.at[at.y, at.x, :, at.c]
        peers = (at.across_xy(), at.across_x(), at.across_y())
        self.waits = [self.net.send(blocks, blocks, peer) for peer in peers]

    def cores(self):
        self.arrive()
        half = self.full.at[:, :, :, self.at.c]
        self.waits = [self.net.send(half, half, self.at.sibling())]


class Direct:
    def __init__(self, net, at, full):
        self.net, self.at, self.full = net, at, full

    def start(self):
        at = self.at
        own = self.full.at[at.y, at.x, at.z, at.c]
        self.waits = [
            self.net.send(own, own, at.dev(*at.other(*way), at.c)) for way in at.others()
        ]

    def arrive(self):
        for copy in self.waits:
            copy.wait_recv()

    def cores(self):
        self.arrive()
        half = self.full.at[:, :, :, self.at.c]
        self.waits = [self.net.send(half, half, self.at.sibling())]


class Owners:
    def __init__(self, net, at, source, target):
        self.net, self.at, self.source, self.target = net, at, source, target
        self.first = net.slots(4)

    def copy(self, k, sender):
        first = self.first
        return self.net.copy(
            self.source(k), self.target(k), self.at.toward(k), first + k, first + sender
        )

    def send(self, k):
        @pl.when(self.at.z != k)
        def _():
            self.copy(k, self.at.z).start()

    def arrive(self):
        for step in (1, 2, 3):
            sender = self.at.ahead(step)
            self.copy(sender, sender).wait_recv()

    def drain(self):
        for step in (1, 2, 3):
            self.copy(self.at.ahead(step), self.at.z).wait_send()


class Relayed:
    def __init__(self, net, at, full):
        self.net, self.at, self.full = net, at, full
        self.zs = at.line()
        self.planes, self.core_moves = [None] * 4, [None] * 4

    def block(self, z):
        at = self.at
        return self.full.at[at.y, at.x, z, at.c]

    def plane(self, k):
        at, block = self.at, self.block(self.zs[k])
        peers = (at.across_xy(), at.across_x(), at.across_y())
        self.planes[k] = [self.net.send(block, block, peer) for peer in peers]

    def send_near(self):
        own = self.block(self.at.z)
        self.near = self.net.send(own, own, self.at.toward(self.zs[1]))

    def send_far(self):
        own = self.block(self.at.z)
        self.far = self.net.send(own, own, self.at.toward(self.zs[2]))

    def take_near(self):
        self.near.wait_recv()
        self.plane(1)

    def take_far(self):
        self.far.wait_recv()
        block = self.block(self.zs[2])
        self.relay = self.net.send(block, block, self.at.toward(self.zs[1]))
        self.plane(2)

    def take_relay(self):
        self.relay.wait_recv()
        self.plane(3)

    def cores(self, k):
        for copy in self.planes[k]:
            copy.wait_recv()
        blocks = self.full.at[:, :, self.zs[k], self.at.c]
        self.core_moves[k] = self.net.send(blocks, blocks, self.at.sibling())

    def done(self):
        for copy in self.core_moves:
            copy.wait_recv()


class Scatter:
    def __init__(self, net, at, part, bufs):
        self.net, self.at, self.part = net, at, part
        self.sums, self.low1, self.high1, self.low2, self.high2, self.last = bufs

    def arrive(self):
        for copy in self.waits:
            copy.wait_recv()

    def cores(self):
        at = self.at
        self.waits = [self.net.send(self.part.at[:, :, :, 1 - at.c], self.sums, at.sibling())]

    def first(self):
        self.arrive()
        at, sums, part = self.at, self.sums, self.part

        def add(i, carry):
            y, x, z = lax.div(i, 8), lax.rem(lax.div(i, 4), 2), lax.rem(i, 4)
            sums[y, x, z] = sums[y, x, z] + part[y, x, z, at.c]
            return carry

        lax.fori_loop(0, 16, add, 0)
        self.waits = [
            self.net.send(sums.at[:, 1 - at.x, 0:2], self.low1, at.across_x()),
            self.net.send(sums.at[1 - at.y, :, 2:4], self.high1, at.across_y()),
        ]

    def second(self):
        self.arrive()
        at, sums = self.at, self.sums

        def add(i, carry):
            a, b = lax.div(i, 2), lax.rem(i, 2)
            sums[a, at.x, b] = sums[a, at.x, b] + self.low1[a, b]
            sums[at.y, a, b + 2] = sums[at.y, a, b + 2] + self.high1[a, b]
            return carry

        lax.fori_loop(0, 4, add, 0)
        self.waits = [
            self.net.send(sums.at[1 - at.y, at.x, 0:2], self.low2, at.across_y()),
            self.net.send(sums.at[at.y, 1 - at.x, 2:4], self.high2, at.across_x()),
        ]

    def gathered(self):
        self.arrive()
        at, sums = self.at, self.sums
        for b in range(2):
            sums[at.y, at.x, b] = sums[at.y, at.x, b] + self.low2[b]
            sums[at.y, at.x, b + 2] = sums[at.y, at.x, b + 2] + self.high2[b]

    def along_z(self):
        self.gathered()
        at, sums = self.at, self.sums
        self.waits = [
            self.net.send(sums.at[at.y, at.x, at.ahead(s)], self.last.at[s - 1], at.along_z(s))
            for s in (1, 2, 3)
        ]

    def pair(self):
        self.gathered()
        at, sums, last = self.at, self.sums, self.last
        near = at.near()
        peer = at.toward(near)
        beyond = sums.at[at.y, at.x, lax.rem(near + 2, 4)]
        self.waits = [self.net.send(beyond, last.at[1], peer)]
        self.near = self.net.send(sums.at[at.y, at.x, near], last.at[0], peer)

    def far(self):
        self.arrive()
        at, sums, last = self.at, self.sums, self.last
        far = at.ahead(2)
        sums[at.y, at.x, far] = sums[at.y, at.x, far] + last[1]
        self.waits = [
            self.near,
            self.net.send(sums.at[at.y, at.x, far], last.at[2], at.toward(far)),
        ]

    def total(self):
        self.arrive()
        at = self.at
        total = self.sums[at.y, at.x, at.z].astype(F32)
        return total + self.last[0].astype(F32) + self.last[2].astype(F32)


class DirectScatter:
    def __init__(self, net, at, part, sums, landed):
        self.net, self.at, self.part, self.sums, self.landed = net, at, part, sums, landed

    def cores(self):
        at = self.at
        self.move = self.net.send(self.part.at[:, :, :, 1 - at.c], self.sums, at.sibling())

    def start(self):
        self.move.wait_recv()
        at, sums = self.at, self.sums
        sums[...] = sums[...] + self.part[:, :, :, at.c]
        self.waits = []
        for i, way in enumerate(at.others()):
            y, x, z = at.other(*way)
            self.waits.append(
                self.net.send(sums.at[y, x, z], self.landed.at[i], at.dev(y, x, z, at.c))
            )

    def total(self):
        at = self.at
        total = self.sums[at.y, at.x, at.z].astype(F32)
        for i, copy in enumerate(self.waits):
            copy.wait_recv()
            total = total + self.landed[i].astype(F32)
        return total


def spread(ref, value, width):
    for j in range(width):
        ref[pl.ds(j, value.shape[0], stride=width), :] = value[:, 128 * j : 128 * j + 128]


def norm_parts(hidden):
    centered = hidden - jnp.mean(hidden, axis=-1, keepdims=True)
    spread_of = jnp.mean(centered * centered, axis=-1, keepdims=True)
    inverse = lax.rsqrt(spread_of + EPSILON)
    return centered * inverse, inverse


def norm_back(upstream, gain_row, normal, inverse):
    scaled = upstream * gain_row
    return inverse * (
        scaled
        - jnp.mean(scaled, axis=-1, keepdims=True)
        - normal * jnp.mean(scaled * normal, axis=-1, keepdims=True)
    )


def column_sum(value):
    return jnp.sum(value, axis=0, keepdims=True)


SHARDS = dict(emb=(48, 128), qkv=(16, 384), out=(16, 512), up=(16, 2048), down=(64, 512))


INPUTS = [
    "stream",
    "ids",
    "cot",
    "emb",
    "qkv",
    "out",
    "up",
    "down",
    "gains",
    "shifts",
    "outs",
    "ubias",
    "rel",
]
LOADS = INPUTS[3:4] + INPUTS[8:] + INPUTS[4:8] + INPUTS[0:3]
OUTPUTS = ["act", "gstream", "o_emb", "o_qkv", "o_out", "o_up", "o_down", "o_small"]


def scratch():
    vm = pltpu.VMEM
    s = dict(
        lin32=vm((256, 128), F32),
        emb32=vm((1024, 128), F32),
        qkv_src=vm((4, 16, 384), BF16),
        small32=vm((512, 128), F32),
        select=vm((3, 128, 512), BF16),
        landed=vm((15, 48, 128), BF16),
        vecs=vm((16, 512), F32),
        rel_row=vm((1, 256), F32),
        bias_row=vm((1, 2048), F32),
        picks=vm((256, 128), BF16),
        start=vm((128, 512), F32),
        normal1=vm((128, 512), F32),
        inverse1=vm((128, 1), F32),
        normed1=vm((4, 128, 512), BF16),
        query=vm((4, 128, 128), BF16),
        keyval=vm((2, 4, 2, 128, 128), BF16),
        probs=vm((2, 128, 2560), F32),
        mixed_out=vm((4, 128, 128), BF16),
        mixed=vm((128, 512), BF16),
        middle=vm((128, 512), F32),
        normal2=vm((128, 512), F32),
        inverse2=vm((128, 1), F32),
        normed2=vm((128, 512), BF16),
        acc1=vm((128, 512), F32),
        acc2=vm((128, 512), F32),
        gub=vm((1, 2048), F32),
        grad_mid=vm((128, 512), F32),
        gmix_src=vm((128, 512), BF16),
        gmix=vm((4, 128, 128), BF16),
        dkv=vm((2, 4, 2, 128, 128), F32),
        dkv_in=vm((2, 4, 128, 128), F32),
        slope=vm((128, 2048), F32),
        active=vm((128, 2048), BF16),
        dproj=vm((4, 128, 384), BF16),
        gnorm=vm((4, 128, 512), BF16),
        gnorm_in=vm((4, 128, 512), BF16),
        sg=vm((16, 512), F32),
        gathered=vm((4, 16, 384), BF16),
    )
    for name, shard in SHARDS.items():
        s["w_" + name] = vm((2, 2, 4, 2) + shard, BF16)
        s["g_" + name] = vm((2, 2, 4, 2) + shard, BF16)
        s["r0_" + name] = vm((2, 2, 4) + shard, BF16)
        s["r1_" + name] = vm((2, 2) + shard, BF16)
        s["r2_" + name] = vm((2, 2) + shard, BF16)
        s["r3_" + name] = vm((2,) + shard, BF16)
        s["r4_" + name] = vm((2,) + shard, BF16)
        s["r5_" + name] = vm((3,) + shard, BF16)
    for name, shape, kind in (
        ("stream", (ROWS, D), BF16),
        ("ids", (1, ROWS), jnp.int32),
        ("cot", (ROWS, D), BF16),
        ("emb", (32, 128), BF16),
        ("qkv", (192, 128), BF16),
        ("out", (64, 128), BF16),
        ("up", (256, 128), BF16),
        ("down", (256, 128), BF16),
        ("gains", (1, 32), BF16),
        ("shifts", (1, 32), BF16),
        ("outs", (1, 32), BF16),
        ("ubias", (1, 64), BF16),
        ("rel", (1, 8), BF16),
    ):
        s[name] = vm(shape, kind)
    s["in_sems"] = pltpu.SemaphoreType.DMA((len(INPUTS),))
    s["send_sems"] = pltpu.SemaphoreType.DMA((240,))
    s["recv_sems"] = pltpu.SemaphoreType.DMA((240,))
    return s


def fused_kernel(*refs):
    hbm = ["h_" + name for name in INPUTS]
    names = hbm + OUTPUTS + list(scratch())
    v = types.SimpleNamespace(**dict(zip(names, refs, strict=True)))
    at = Place()
    net = Net(v.send_sems, v.recv_sems)
    y, x, z, c = at.y, at.x, at.z, at.c

    barrier = pltpu.get_barrier_semaphore()
    peers = [at.dev(*at.other(*way), c) for way in at.others()] + [at.sibling()]
    for peer in peers:
        pl.semaphore_signal(
            barrier, inc=1, device_id=peer, device_id_type=pl.DeviceIdType.MESH
        )
    loads = {}
    for i, name in enumerate(LOADS):
        loads[name] = pltpu.make_async_copy(
            getattr(v, "h_" + name), getattr(v, name), v.in_sems.at[i]
        )
        loads[name].start()

    for name in ("emb", "gains", "shifts", "outs", "ubias", "rel"):
        loads[name].wait()
    v.small32[...] = jnp.zeros((512, 128), F32)
    for i, piece in enumerate((v.gains, v.shifts, v.outs, v.ubias, v.rel)):
        v.small32[i : i + 1, 0 : piece.shape[1]] = piece[...].astype(F32)
    v.w_emb[y, x, z, c, 0:32] = v.emb[...]
    v.w_emb[y, x, z, c, 32:48] = v.small32[0:16, :].astype(BF16)
    pl.semaphore_wait(barrier, len(peers))
    emb = Direct(net, at, v.w_emb)
    emb.start()

    loads["qkv"].wait()
    v.lin32[0:192, :] = v.qkv[...].astype(F32)
    for t in range(3):
        for zz in range(4):
            piece = v.lin32[pl.ds(4 * t + zz, 16, stride=12), :].astype(BF16)
            v.qkv_src[zz, :, 128 * t : 128 * t + 128] = piece
    v.w_qkv[y, x, z, c] = v.qkv_src[z]
    qkv = Columns(net, at, v.w_qkv, v.qkv_src)
    qkv.along_z()
    slow = []
    for name, rows, width in (("out", 16, 4), ("up", 16, 16), ("down", 64, 4)):
        loads[name].wait()
        full = getattr(v, "w_" + name)
        v.lin32[0 : rows * width, :] = getattr(v, name)[...].astype(F32)
        for j in range(width):
            full[y, x, z, c, :, 128 * j : 128 * j + 128] = v.lin32[
                pl.ds(j, rows, stride=width), :
            ].astype(BF16)
        slow.append(Relayed(net, at, full))
        if name != "down":
            slow[-1].send_near()
            slow[-1].send_far()
        slow[-1].plane(0)
    out, up, down = slow

    lane = lax.broadcasted_iota(jnp.int32, (128, 512), 1)
    row = lax.broadcasted_iota(jnp.int32, (128, 512), 0)
    for i, size in enumerate((32, 64, 8)):
        v.select[i] = (lax.rem(lane, size) == row).astype(F32).astype(BF16)
    loads["ids"].wait()
    v.picks[...] = (
        (lax.broadcasted_iota(jnp.int32, (VOCAB, ROWS), 0) == v.ids[...]).astype(F32).astype(BF16)
    )
    emb.cores()
    loads["stream"].wait()
    loads["cot"].wait()
    emb.arrive()

    v.emb32[...] = v.w_emb[:, :, :, :, 0:32, :].reshape(1024, 128).astype(F32)
    v.small32[...] = v.w_emb[:, :, :, :, 32:48, :].reshape(512, 128).astype(F32)
    owner = lax.broadcasted_iota(jnp.int32, (32, 512), 0)
    where = lax.broadcasted_iota(jnp.int32, (32, 512), 1)

    def tiled(kind, select):
        pieces = v.small32[pl.ds(kind, 32, stride=16), :].astype(BF16)
        return dot_nn(pieces, v.select[select])

    def picked(wide, size, first):
        return column_sum(jnp.where(owner == first + lax.div(where, size), wide, 0.0))

    def halves(kind):
        wide = tiled(kind, 0)
        for half in range(2):
            v.vecs[2 * kind + half : 2 * kind + half + 1, :] = picked(wide, 32, 16 * half)

    halves(0)
    halves(1)
    for j in range(4):
        cut = slice(128 * j, 128 * j + 128)
        table = v.emb32[pl.ds(j, VOCAB, stride=4), :].astype(BF16)
        v.start[:, cut] = v.stream[:, cut].astype(F32) + dot_tn(v.picks[...], table)
    normal, inverse = norm_parts(v.start[...])
    v.normal1[...] = normal
    v.inverse1[...] = inverse
    v.normed1[z] = (normal * v.vecs[0:1, :] + v.vecs[2:3, :]).astype(BF16)
    line = at.line()
    own = v.normed1.at[z]
    halves_of = [pl.ds(0, 64), pl.ds(64, 64)]
    normed_near = net.send(own, own, at.toward(line[1]))
    normed_far = [
        net.send(v.normed1.at[z, part], v.normed1.at[z, part], at.toward(line[2]))
        for part in halves_of
    ]
    qkv.plane()
    out.take_near()
    up.take_near()
    halves(2)
    wide = tiled(3, 1)
    for block in range(4):
        v.bias_row[:, 512 * block : 512 * block + 512] = picked(wide, 64, 8 * block)
    rel_row = picked(tiled(4, 2), 8, 0)[:, 0:256]
    rel_lane = lax.broadcasted_iota(jnp.int32, (1, 256), 1)
    out.take_far()
    up.take_far()
    down.send_near()
    for g in (out, up, down):
        g.cores(0)
    qkv.cores()

    qkv.arrive()
    weight = v.w_qkv[...].reshape(512, 384)
    moves = []

    def project(zs):
        projected = dot_nn(v.normed1[zs], weight).astype(BF16)
        v.query[zs] = projected[:, 0:128]
        v.keyval[0, zs, c] = projected[:, 128:256]
        v.keyval[1, zs, c] = projected[:, 256:384]
        both = v.keyval.at[:, zs, c]
        moves.append(net.send(both, both, at.sibling()))

    project(z)
    normed_relay = []
    for i, part in enumerate(halves_of):
        normed_far[i].wait_recv()
        piece = v.normed1.at[line[2], part]
        normed_relay.append(net.send(piece, piece, at.toward(line[1])))
    down.send_far()
    normed_near.wait_recv()
    project(line[1])
    project(line[2])
    out.take_relay()
    up.take_relay()
    out.cores(1)
    up.cores(1)
    for copy in normed_relay:
        copy.wait_recv()
    project(line[3])
    down.take_near()
    for copy in moves:
        copy.wait_recv()

    pair_lane = lax.broadcasted_iota(jnp.int32, (ROWS, PAIR), 1)
    head_lanes = (pair_lane < HEAD_DIM, pair_lane >= HEAD_DIM)

    def rel_value(head, distance):
        spot = (2 * z + head) * BUCKETS + distance
        return jnp.sum(jnp.where(rel_lane == spot, rel_row, 0.0), axis=1, keepdims=True)

    rel_values = [[rel_value(h, d) for d in range(4)] for h in range(2)]
    zero = jnp.zeros((), BF16)
    own_lanes = pl.ds(pl.multiple_of(z * PAIR, PAIR), PAIR)
    to_owner = Owners(net, at, lambda k: v.mixed_out.at[k], lambda k: v.mixed.at[:, own_lanes])
    for zq in range(4):
        count = 256 * (zq + 1)
        keys = v.keyval[0, 0 : zq + 1].reshape(count, PAIR)
        vals = v.keyval[1, 0 : zq + 1].reshape(count, PAIR)
        heads = []
        for h in range(2):
            query = jnp.where(head_lanes[h], v.query[zq], zero)
            bias = jnp.concatenate(
                [
                    jnp.broadcast_to(rel_values[h][zq - zk], (1, 256))
                    for zk in range(zq + 1)
                ],
                axis=1,
            )
            scores = dot_nt(query, keys) * SCALING + bias
            shifted = jnp.exp(scores - jnp.max(scores, axis=-1, keepdims=True))
            probs = shifted / jnp.sum(shifted, axis=-1, keepdims=True)
            v.probs[h, :, KEYS_AT[zq] : KEYS_AT[zq] + count] = probs
            heads.append(dot_nn(probs.astype(BF16), vals))
        v.mixed_out[zq] = jnp.where(head_lanes[0], heads[0], heads[1]).astype(BF16)
        to_owner.send(zq)
    v.mixed[:, own_lanes] = v.mixed_out[z]
    for k in (2, 3):
        out.cores(k)
        up.cores(k)
    down.take_far()
    down.cores(1)
    down.take_relay()
    to_owner.arrive()

    out.done()
    mixed = v.mixed[...]
    out_weight = v.w_out[...].reshape(512, 512)
    middle = v.start[...] + dot_nn(mixed, out_weight) + v.vecs[4:5, :]
    v.middle[...] = middle
    normal, inverse = norm_parts(middle)
    v.normal2[...] = normal
    v.inverse2[...] = inverse
    v.normed2[...] = (normal * v.vecs[1:2, :] + v.vecs[3:4, :]).astype(BF16)
    v.acc1[...] = jnp.zeros_like(v.acc1)
    v.acc2[...] = jnp.zeros_like(v.acc2)
    down.cores(2)
    up.done()

    def scatter(name):
        bufs = [getattr(v, f"r{i}_{name}") for i in range(6)]
        return Scatter(net, at, getattr(v, "g_" + name), bufs)

    s_down, s_up, s_out, s_qkv = (scatter(n) for n in ("down", "up", "out", "qkv"))
    s_emb = DirectScatter(net, at, v.g_emb, v.r0_emb, v.landed)

    def forward_tile(i, carry):
        cols = pl.ds(pl.multiple_of(i * 256, 256), 256)
        ty, tx, tz = lax.div(i, 4), lax.rem(lax.div(i, 2), 2), lax.rem(i, 2) * 2
        up_tile = v.w_up[:, :, :, :, :, cols].reshape(512, 256)
        lifted = dot_nn(v.normed2[...], up_tile) + v.bias_row[:, cols]
        share = 0.5 * (1.0 + lax.erf(lifted * ROOT_HALF))
        active = (lifted * share).astype(BF16)
        v.active[:, cols] = active
        v.slope[:, cols] = share + lifted * (jnp.exp(-0.5 * lifted * lifted) * ROOT_TAU)
        v.g_down[ty, tx, pl.ds(tz, 2)] = (
            dot_tn(active, v.cot[...]).astype(BF16).reshape(2, 2, 64, 512)
        )
        return carry

    lax.fori_loop(0, 8, forward_tile, 0, unroll=2)
    s_down.cores()
    down.cores(3)
    down.done()

    def backward_tile(i, carry):
        cols = pl.ds(pl.multiple_of(i * 256, 256), 256)
        ty, tx, tz = lax.div(i, 4), lax.rem(lax.div(i, 2), 2), lax.rem(i, 2) * 2
        up_tile = v.w_up[:, :, :, :, :, cols].reshape(512, 256)
        down_tile = v.w_down[ty, tx, pl.ds(tz, 2)].reshape(256, 512)
        v.acc1[...] += dot_nn(v.active[:, cols], down_tile)
        grad_lifted = dot_nt(v.cot[...], down_tile) * v.slope[:, cols]
        v.gub[:, cols] = column_sum(grad_lifted)
        low = grad_lifted.astype(BF16)
        v.acc2[...] += dot_nt(low, up_tile)
        v.g_up[:, :, :, :, :, cols] = (
            dot_tn(v.normed2[...], low).astype(BF16).reshape(2, 2, 4, 2, 16, 256)
        )
        return carry

    lax.fori_loop(0, 4, backward_tile, 0, unroll=2)
    s_down.first()
    lax.fori_loop(4, 8, backward_tile, 0, unroll=2)
    s_up.cores()
    grad_wide = v.cot[...].astype(F32)
    upstream = v.acc2[...]
    normal = v.normal2[...]
    grad_middle = grad_wide + norm_back(upstream, v.vecs[1:2, :], normal, v.inverse2[...])
    v.grad_mid[...] = grad_middle
    middle_low = grad_middle.astype(BF16)
    v.gmix_src[...] = dot_nt(middle_low, v.w_out[...].reshape(512, 512)).astype(BF16)
    moves = [
        net.send(
            v.gmix_src.at[:, pl.ds(pl.multiple_of(at.ahead(s) * PAIR, PAIR), PAIR)],
            v.gmix.at[z],
            at.along_z(s),
        )
        for s in (1, 2, 3)
    ]
    v.gmix[z] = v.gmix_src[:, own_lanes]
    v.g_out[...] = dot_tn(v.mixed[...], middle_low).astype(BF16).reshape(2, 2, 4, 2, 16, 512)
    s_out.cores()
    v.sg[1:2, :] = column_sum(upstream * normal)
    v.sg[3:4, :] = column_sum(upstream)
    v.sg[4:5, :] = column_sum(grad_middle)
    v.sg[5:6, :] = column_sum(grad_wide)
    v.act[...] = (v.middle[...] + v.acc1[...] + v.vecs[5:6, :]).astype(BF16)
    s_up.first()
    s_out.first()
    for copy in moves:
        copy.wait_recv()

    rel_sums = [[jnp.zeros((1, 256), F32) for d in range(4)] for h in range(2)]
    weight = v.w_qkv[...].reshape(512, 384)
    core_moves = {}
    gnorm_out = Owners(net, at, lambda k: v.gnorm.at[k], lambda k: v.gnorm_in.at[z])

    def project_back(zq):
        core_moves[zq].wait_recv()
        dkeys = (v.dkv[0, zq, c] + v.dkv_in[0, zq]) * SCALING
        dvals = v.dkv[1, zq, c] + v.dkv_in[1, zq]
        v.dproj[zq, :, 128:256] = dkeys.astype(BF16)
        v.dproj[zq, :, 256:384] = dvals.astype(BF16)
        v.gnorm[zq] = dot_nt(v.dproj[zq], weight).astype(BF16)
        gnorm_out.send(zq)

    for zq in (3, 2, 1, 0):
        count = 256 * (zq + 1)
        keys = v.keyval[0, 0 : zq + 1].reshape(count, PAIR)
        vals = v.keyval[1, 0 : zq + 1].reshape(count, PAIR)
        heads, dkeys, dvals = [], 0.0, 0.0
        for h in range(2):
            query = jnp.where(head_lanes[h], v.query[zq], zero)
            grad = jnp.where(head_lanes[h], v.gmix[zq], zero)
            probs = v.probs[h, :, KEYS_AT[zq] : KEYS_AT[zq] + count]
            grad_probs = dot_nt(grad, vals)
            inner = jnp.sum(probs * grad_probs, axis=-1, keepdims=True)
            grad_scores = probs * (grad_probs - inner)
            for zk in range(zq + 1):
                tile = grad_scores[:, 256 * zk : 256 * zk + 256]
                rel_sums[h][zq - zk] = rel_sums[h][zq - zk] + column_sum(tile)
            low = grad_scores.astype(BF16)
            heads.append(dot_nn(low, keys))
            dkeys = dkeys + dot_tn(low, query)
            dvals = dvals + dot_tn(probs.astype(BF16), grad)
        v.dproj[zq, :, 0:128] = (
            jnp.where(head_lanes[0], heads[0], heads[1]) * SCALING
        ).astype(BF16)
        dkeys = dkeys.reshape(zq + 1, 2, ROWS, PAIR)
        dvals = dvals.reshape(zq + 1, 2, ROWS, PAIR)
        if zq == 3:
            v.dkv[0] = dkeys
            v.dkv[1] = dvals
        else:
            v.dkv[0, 0 : zq + 1] += dkeys
            v.dkv[1, 0 : zq + 1] += dvals
        core_moves[zq] = net.send(
            v.dkv.at[:, zq, 1 - c], v.dkv_in.at[:, zq], at.sibling()
        )
        if zq < 3:
            project_back(zq + 1)
        if zq == 3:
            s_down.second()
    project_back(0)
    s_up.second()
    s_out.second()
    v.g_qkv[...] = (
        dot_tn(v.normed1[...].reshape(512, 512), v.dproj[...].reshape(512, 384))
        .astype(BF16)
        .reshape(2, 2, 4, 2, 16, 384)
    )
    s_qkv.cores()
    s_down.pair()
    s_up.pair()
    s_out.pair()

    sums = jnp.zeros((1, 512), F32)
    wide_lane = lax.broadcasted_iota(jnp.int32, (1, 512), 1)
    for h in range(2):
        for d in range(4):
            spot = (2 * z + h) * BUCKETS + d
            value = jnp.sum(rel_sums[h][d], axis=1, keepdims=True)
            sums = sums + jnp.where(wide_lane == spot, value, 0.0)

    def cut(kind, select, size, lines):
        wide = jnp.zeros((32, 512), F32)
        for i, line in enumerate(lines):
            first = (512 // size) * i
            wide = jnp.where(owner == first + lax.div(where, size), line, wide)
        v.small32[pl.ds(kind, 32, stride=16), :] = dot_nt(wide.astype(BF16), v.select[select])

    v.small32[...] = jnp.zeros((512, 128), F32)
    cut(2, 0, 32, [v.sg[4:5, :], v.sg[5:6, :]])
    cut(3, 1, 64, [v.gub[:, 512 * i : 512 * i + 512] for i in range(4)])
    cut(4, 2, 8, [sums])
    s_qkv.first()

    gnorm_out.arrive()
    upstream = v.gnorm[z].astype(F32)
    for s in (1, 2, 3):
        upstream = upstream + v.gnorm_in[at.ahead(s)].astype(F32)
    normal = v.normal1[...]
    grad_start = v.grad_mid[...] + norm_back(upstream, v.vecs[0:1, :], normal, v.inverse1[...])
    start_low = grad_start.astype(BF16)
    spread(v.emb32, dot_nn(v.picks[...], start_low), 4)
    v.g_emb[:, :, :, :, 0:32, :] = v.emb32[...].astype(BF16).reshape(2, 2, 4, 2, 32, 128)
    cut(0, 0, 32, [column_sum(upstream * normal), v.sg[1:2, :]])
    cut(1, 0, 32, [column_sum(upstream), v.sg[3:4, :]])
    v.g_emb[:, :, :, :, 32:48, :] = v.small32[...].astype(BF16).reshape(2, 2, 4, 2, 16, 128)
    s_emb.cores()
    v.gstream[...] = start_low
    s_emb.start()
    s_down.far()
    s_qkv.second()
    s_up.far()
    s_out.far()
    s_qkv.along_z()
    spread(v.o_down, s_down.total(), 4)
    total = s_emb.total()
    v.o_emb[...] = total[0:32]
    v.o_small[...] = total[32:40]
    spread(v.o_up, s_up.total(), 16)
    spread(v.o_out, s_out.total(), 4)
    s_qkv.arrive()
    v.gathered[z] = v.r0_qkv[y, x, z]
    for s in (1, 2, 3):
        v.gathered[at.behind(s)] = v.r5_qkv[s - 1]
    for zz in range(4):
        piece = v.gathered[zz].astype(F32)
        for t in range(3):
            v.o_qkv[pl.ds(4 * t + zz, 16, stride=12), :] = piece[:, 128 * t : 128 * t + 128]
    to_owner.drain()
    gnorm_out.drain()
    net.drain()


def store_kernel(*refs):
    ins, small, outs, sems = refs[:7], refs[7], refs[8:20], refs[20]
    copies = [pltpu.make_async_copy(ins[i], outs[i], sems.at[i]) for i in range(7)]
    for copy in copies:
        copy.start()
    for i in range(5):
        outs[7 + i][...] = small[i : i + 1, 0 : outs[7 + i].shape[1]]
    for copy in copies:
        copy.wait()


def fused_local(
    stream,
    byte_ids,
    cotangent,
    embed_flat,
    qkv_flat,
    out_flat,
    up_flat,
    down_flat,
    gains,
    norm_shifts,
    out_shifts,
    up_bias,
    rel_bias,
):
    operands = (
        stream.reshape(ROWS, D),
        byte_ids,
        cotangent.reshape(ROWS, D),
        embed_flat.reshape(-1, 128),
        qkv_flat.reshape(-1, 128),
        out_flat.reshape(-1, 128),
        up_flat.reshape(-1, 128),
        down_flat.reshape(-1, 128),
        gains.reshape(1, -1),
        norm_shifts.reshape(1, -1),
        out_shifts.reshape(1, -1),
        up_bias.reshape(1, -1),
        rel_bias.reshape(1, -1),
    )
    shapes = (
        ((ROWS, D), BF16),
        ((ROWS, D), BF16),
        ((32, 128), F32),
        ((192, 128), F32),
        ((64, 128), F32),
        ((256, 128), F32),
        ((256, 128), F32),
        ((8, 128), F32),
    )
    whole = pl.BlockSpec(memory_space=pltpu.VMEM)
    anywhere = pl.BlockSpec(memory_space=pl.ANY)
    results = pl.pallas_call(
        fused_kernel,
        out_shape=[pltpu.VMEM(s, t) for s, t in shapes],
        in_specs=[pl.BlockSpec(memory_space=pltpu.HBM)] * len(operands),
        out_specs=[whole] * len(shapes),
        scratch_shapes=list(scratch().values()),
        compiler_params=pltpu.CompilerParams(
            collective_id=0, has_side_effects=True, vmem_limit_bytes=32 << 20
        ),
        name="layer",
    )(*(pltpu.with_memory_space_constraint(o, pltpu.HBM) for o in operands))
    vectors = (gains, norm_shifts, out_shifts, up_bias, rel_bias)
    small_shapes = [((1, p.shape[0]), F32) for p in vectors]
    final = pl.pallas_call(
        store_kernel,
        out_shape=[jax.ShapeDtypeStruct(s, t) for s, t in shapes[:7] + tuple(small_shapes)],
        in_specs=[whole] * 8,
        out_specs=[anywhere] * 7 + [whole] * 5,
        scratch_shapes=[pltpu.SemaphoreType.DMA((7,))],
        compiler_params=pltpu.CompilerParams(vmem_limit_bytes=8 << 20),
        name="store",
    )(*results)
    return (
        final[0].reshape(stream.shape),
        final[1].reshape(stream.shape),
        *(part.reshape(-1) for part in final[2:]),
    )


def solution(mesh):
    body = fused_local if (mesh.shape["dp"], mesh.shape["seq"]) == (4, 8) else local
    in_specs = (
        P("dp", "seq", None),
        P("dp", "seq"),
        P("dp", "seq", None),
        P(("dp", "seq")),
        P(("dp", "seq")),
        P(("dp", "seq")),
        P(("dp", "seq")),
        P(("dp", "seq")),
        P(("dp", "seq")),
        P(("dp", "seq")),
        P(("dp", "seq")),
        P(("dp", "seq")),
        P(("dp", "seq")),
    )
    out_specs = (
        P("dp", "seq", None),
        P("dp", "seq", None),
        P(("dp", "seq")),
        P(("dp", "seq")),
        P(("dp", "seq")),
        P(("dp", "seq")),
        P(("dp", "seq")),
        P(("dp", "seq")),
        P(("dp", "seq")),
        P(("dp", "seq")),
        P(("dp", "seq")),
        P(("dp", "seq")),
    )
    return jax.shard_map(body, mesh=mesh, in_specs=in_specs, out_specs=out_specs, check_vma=False)
```
